256 devices in a mesh: tm: 8 (over x, core), space: 32 (over z, y).
Axes of the slice: x: 4, y: 4, z: 8, core: 2. Of those that a mesh axis runs over, the one named last changes fastest.
Arguments:
- guesses: float32 [8, 512, 4096], P('tm', 'space'), may hold values from -6 to 6
- cond_x: float32 [512, 4096], P('space'), may hold values from 0.025 to 0.24
- cond_y: float32 [512, 4096], P('space'), may hold values from 0.005 to 0.05
- source: float32 [512, 4096], P('space'), may hold values from -0.6 to 0.6
- inflow: float32 [256, 2048], P('space'), may hold values from -6 to 6
Outputs:
- corrected: float32 [8, 512, 4096], P('tm', 'space')
The draws below stay inside these ranges and needn't reach their ends.
All inputs are finite; a program needn't handle non-finite values.
Results may differ from the reference program's by a relative error of at most 0.00002.
Values sent between devices are 32-bit elements; how exact they have to be, the bound alone decides.
A program may use at most 128 MiB of HBM per device.

```python
import math
import jax
import jax.numpy as jnp
from jax import lax

NY = 4096
FINE_STEPS = 4
GROUPS = 8
NX = 512


def level_of(own_key, shape, pieces, smallest, high):
    loudness, own = 1.0, jax.random.fold_in(own_key, 6)
    for dim, shards_of in pieces:
        heights = jnp.exp(jax.random.uniform(jax.random.fold_in(own, dim), (shards_of,), jnp.float32, smallest / len(pieces), high / len(pieces)))
        loudness = loudness * jnp.repeat(heights, shape[dim] // shards_of).reshape([-1 if axis == dim else 1 for axis in range(len(shape))])
    return loudness


def gaussian(own_key, extent, spread, limit, pieces=(), kind=jnp.bfloat16):
    array = jax.random.normal(own_key, extent, jnp.float32) * spread
    if len(pieces) > 0:
        array = level_of(own_key, extent, pieces, -0.22, 0.18) * array
    return jnp.clip(array, min=-limit, max=limit).astype(kind)


def setup_inputs(seed: int = 0) -> dict:
    arg_keys = jax.random.split(jax.random.key(seed), 6)
    return {
        "guesses": gaussian(arg_keys[0], (GROUPS, NX, NY), 1.0, 6.0, ((0, 8), (1, 32)), jnp.float32),
        "cond_x": jnp.clip(jnp.exp(math.log(0.24) - 2.261763 * jax.random.uniform(arg_keys[1], (NX, NY), jnp.float32) ** level_of(arg_keys[1], (NX, NY), ((0, 32),), -0.2, 0.2)), 0.025, 0.24),
        "cond_y": jnp.clip(jnp.exp(math.log(0.05) - 2.3025851 * jax.random.uniform(arg_keys[2], (NX, NY), jnp.float32) ** level_of(arg_keys[2], (NX, NY), ((0, 32),), -0.2, 0.2)), 0.005, 0.05),
        "source": gaussian(arg_keys[3], (NX, NY), 0.1, 0.6, ((0, 32),), jnp.float32),
        "inflow": gaussian(arg_keys[4], (NX // 2, NY // 2), 1.0, 6.0, ((0, 32),), jnp.float32),
    }


def fine_step(field, cond_x, cond_y, source):
    rows_pad = jnp.pad(field, ((1, 1), (0, 0)))
    cond_prev = jnp.pad(cond_x, ((1, 0), (0, 0)))[:-1]
    flux_sum = cond_x * (rows_pad[2:] - field) - cond_prev * (field - rows_pad[:-2])
    cols_pad = jnp.pad(field, ((0, 0), (1, 1)))
    cond_west = jnp.pad(cond_y, ((0, 0), (1, 0)))[:, :-1]
    flux_sum = flux_sum + cond_y * (cols_pad[:, 2:] - field) - cond_west * (field - cols_pad[:, :-2])
    return field + flux_sum + source


def restrict(field):
    lead = field.shape[:-2]
    shaped = field.reshape(lead + (field.shape[-2] // 2, 2, field.shape[-1] // 2, 2))
    return jnp.mean(shaped, axis=(-3, -1))


def reference(guesses, cond_x, cond_y, source, inflow):
    def propagate(field):
        for section in range(FINE_STEPS):
            field = fine_step(field, cond_x, cond_y, source)
        return field

    first_pass = lax.map(propagate, guesses)
    relaxed = jnp.concatenate([guesses[:1], first_pass[:-1]], axis=0)
    second_pass = lax.map(propagate, relaxed)
    residual = lax.map(restrict, second_pass[:-1] - relaxed[1:])
    coarse_x = restrict(cond_x)
    coarse_y = restrict(cond_y)
    error_field = inflow.astype(jnp.float32)
    errors = [error_field]
    for group in range(1, GROUPS):
        error_field = fine_step(error_field, coarse_x, coarse_y, 0.0) + residual[group - 1]
        errors.append(error_field)
    stacked = jnp.stack(errors)
    widened = jnp.repeat(jnp.repeat(stacked, 2, axis=1), 2, axis=2)
    return relaxed + widened
```

```python
import functools

import jax
import jax.numpy as jnp
from jax import lax
from jax.experimental import pallas as pl
from jax.experimental.pallas import tpu as pltpu
from jax.sharding import PartitionSpec as P

MESH = pl.DeviceIdType.MESH
F32 = jnp.float32
L = 128
TOP = 16


def remote(src, dst, send, recv, where):
    return pltpu.make_async_remote_copy(
        src_ref=src, dst_ref=dst, send_sem=send, recv_sem=recv, device_id=where, device_id_type=MESH
    )


def lane_index():
    return lax.broadcasted_iota(jnp.int32, (8, L), 1)


def gather_lanes(value, index):
    return jnp.take_along_axis(value, index, axis=1, mode="promise_in_bounds")


def restrict_block(ref, block, row, lane):
    halves = []
    for q in range(2):
        pair = ref[2 * block + q, pl.ds(row, 8, stride=2), :] + ref[
            2 * block + q, pl.ds(row + 1, 8, stride=2), :
        ]
        pair = pair + pltpu.roll(pair, L - 1, 1)
        halves.append(gather_lanes(pair, (2 * lane) % L))
    return jnp.where(lane < L // 2, halves[0], halves[1]) * 0.25


def fluxes(u, right, up, down, cx, cx_up, cy, carry, lane):
    flow = cy * (right - u)
    turned = pltpu.roll(flow, 1, 1)
    west = jnp.where(lane == 0, carry, turned)
    total = cx * (down - u) - cx_up * (u - up)
    return total + flow - west, turned


def fine_step(src, dst, cx, cy, source, first, tiles, last_strip, blocks, unroll=4):
    lane = lane_index()
    row = lax.broadcasted_iota(jnp.int32, (8, L), 0)
    rows = [first + 8 * k for k in range(tiles)]
    outside = [None if r + 8 <= TOP + 16 else (row + r >= TOP + 16) & last_strip for r in rows]

    def body(b, carry):
        new = []
        for k, r in enumerate(rows):
            u, ru, turned = carry[k]
            nxt = src[b + 1, r : r + 8, :]
            rn = pltpu.roll(nxt, L - 1, 1)
            right = jnp.where(lane == L - 1, rn, ru)
            change, turned = fluxes(
                u, right, src[b, r - 1 : r + 7, :], src[b, r + 1 : r + 9, :],
                cx[b, r : r + 8, :], cx[b, r - 1 : r + 7, :], cy[b, r : r + 8, :], turned, lane,
            )
            out = u + change + source[b, r : r + 8, :]
            if outside[k] is not None:
                out = jnp.where(outside[k], 0.0, out)
            dst[b, r : r + 8, :] = out
            new.append((nxt, rn, turned))
        return tuple(new)

    start = []
    for r in rows:
        u = src[0, r : r + 8, :]
        start.append((u, pltpu.roll(u, L - 1, 1), jnp.zeros((8, L), F32)))
    lax.fori_loop(0, blocks, body, tuple(start), unroll=unroll)


def kernel(
    groups, strips, guess_in, cx_in, cy_in, source_in, inflow_in, out_hbm,
    stage, flow_stage, own, u0, u1, u2, cx, cy, source, rcx, rcy, inflow, tcoarse, dwin,
    wsrc, win, fa, fb, rd, fsend, frecv, out,
    in_sems, out_sem, a_send, a_recv, w_send, w_recv, d_send, d_recv, f_send, f_recv,
):
    t = lax.axis_index("tm")
    s = lax.axis_index("space")
    even = lax.rem(t, 2) == 0
    has_up, has_down = s > 0, s < strips - 1
    last_t = groups - 1
    lane = lane_index()
    zero = jnp.zeros((8, L), F32)

    loads = [
        pltpu.make_async_copy(ref, stage.at[i], in_sems.at[i])
        for i, ref in enumerate((guess_in.at[0], cx_in, cy_in, source_in))
    ]
    loads.append(pltpu.make_async_copy(inflow_in, flow_stage, in_sems.at[4]))
    for load in loads:
        load.start()

    barrier = pltpu.get_barrier_semaphore()
    for k in range(1, groups):
        pl.semaphore_signal(barrier, inc=1, device_id=(lax.rem(t + k, groups), s), device_id_type=MESH)

    @pl.when(has_up)
    def _():
        for k in range(groups):
            pl.semaphore_signal(barrier, inc=1, device_id=(lax.rem(t + k, groups), s - 1), device_id_type=MESH)

    @pl.when(has_down)
    def _():
        for k in range(groups):
            pl.semaphore_signal(barrier, inc=1, device_id=(lax.rem(t + k, groups), s + 1), device_id_type=MESH)

    near = 3 - jnp.where(has_up, 0, 1) - jnp.where(has_down, 0, 1)

    for load in loads:
        load.wait()
    blocks = own.shape[0]
    cblocks = blocks // 2
    for b in range(blocks):
        cols = slice(b * L, (b + 1) * L)
        own[b, :, :] = stage[0, :, cols]
        cx[b, TOP : TOP + 16, :] = stage[1, :, cols]
        cy[b, TOP : TOP + 16, :] = stage[2, :, cols]
        source[b, TOP : TOP + 16, :] = stage[3, :, cols]
    pl.semaphore_wait(barrier, groups * near - 1)

    up_rows, down_rows, main_rows = slice(TOP - 8, TOP), slice(TOP + 16, TOP + 24), slice(TOP, TOP + 16)
    ahead = lax.rem(t + 1, groups)
    mate = jnp.where(even, t + 1, t - 1)
    coefs = (cx, cy, source)
    sends = []
    inner = u0.at[0:blocks]

    def send(cond, copy):
        sends.append((cond, copy))

        @pl.when(cond)
        def _():
            copy.start()

    for i, ref in enumerate(coefs):
        send(even & has_down, remote(ref.at[:, TOP + 8 : TOP + 16, :], ref.at[:, up_rows, :], a_send.at[i], a_recv.at[i], (t, s + 1)))
        send(~even & has_up, remote(ref.at[:, TOP : TOP + 8, :], ref.at[:, down_rows, :], a_send.at[3 + i], a_recv.at[3 + i], (t, s - 1)))
    guess_down, guess_up = own.at[:, 8:16, :], own.at[:, 0:8, :]
    send((t < last_t) & has_down, remote(guess_down, inner.at[:, up_rows, :], a_send.at[6], a_recv.at[6], (ahead, s + 1)))
    send((t < last_t) & has_up, remote(guess_up, inner.at[:, down_rows, :], a_send.at[7], a_recv.at[7], (ahead, s - 1)))
    send(t < last_t, remote(own, inner.at[:, main_rows, :], a_send.at[8], a_recv.at[8], (ahead, s)))
    send((t == 0) & has_down, remote(guess_down, inner.at[:, up_rows, :], a_send.at[9], a_recv.at[6], (t, s + 1)))
    send((t == 0) & has_up, remote(guess_up, inner.at[:, down_rows, :], a_send.at[10], a_recv.at[7], (t, s - 1)))

    for ref in (rcx, rcy, inflow):
        rows = ref.shape[1]
        for r in range(0, rows, 8):
            ref[0, r : r + 8, :] = zero
            ref[cblocks + 1, r : r + 8, :] = zero
    for b in range(cblocks):
        inflow[b + 1, :, :] = flow_stage[:, b * L : (b + 1) * L]

    def coarse_coefs(b, c):
        rcx[b + 1, 8:16, :] = restrict_block(cx, b, TOP, lane)
        rcy[b + 1, 8:16, :] = restrict_block(cy, b, TOP, lane)
        return c

    lax.fori_loop(0, cblocks, coarse_coefs, 0)

    def shifted(ref, rows):
        turned = [pltpu.roll(ref[2 * t + i, rows, :], L // 2, 1) for i in range(4)]
        return [jnp.where(lane < L // 2, turned[i], turned[i + 1]) for i in range(3)]

    for a, (ref, rows) in enumerate(((inflow, slice(0, 8)), (rcx, slice(8, 16)), (rcy, slice(8, 16)))):
        for i, value in enumerate(shifted(ref, rows)):
            wsrc[a, i, :, :] = value
            win[a, i, 16:24, :] = value
    send(has_down, remote(wsrc, win.at[:, :, 8:16, :], w_send.at[0], w_recv.at[0], (t, s + 1)))
    send(has_up, remote(wsrc, win.at[:, :, 24:32, :], w_send.at[1], w_recv.at[1], (t, s - 1)))

    def clear(ref, rows):
        def body(b, c):
            ref[b, rows, :] = zero
            return c

        lax.fori_loop(0, ref.shape[0], body, 0)

    for ref in (u0, u1, u2):
        for r in range(0, ref.shape[1], 8):
            ref[blocks, r : r + 8, :] = zero

    @pl.when(~has_up)
    def _():
        for ref in (cx, cy, source):
            clear(ref, up_rows)
        clear(inner, up_rows)
        for i in range(3):
            for a in range(3):
                win[a, i, 8:16, :] = zero
            for j in range(last_t):
                rd[j, i, 0:8, :] = zero

    @pl.when(~has_down)
    def _():
        for ref in (cx, cy, source):
            clear(ref, down_rows)
        clear(inner, down_rows)
        for i in range(3):
            for a in range(3):
                win[a, i, 24:32, :] = zero
            for j in range(last_t):
                rd[j, i, 16:24, :] = zero

    @pl.when(t == 0)
    def _():
        for b in range(blocks):
            u0[b, main_rows, :] = own[b, :, :]

    for i, ref in enumerate(coefs):
        upper, lower = ref.at[:, up_rows, :], ref.at[:, down_rows, :]
        up_copy = remote(upper, upper, a_send.at[11 + i], a_recv.at[i], (mate, s))
        down_copy = remote(lower, lower, a_send.at[14 + i], a_recv.at[3 + i], (mate, s))

        @pl.when(even & has_up)
        def _(up_copy=up_copy):
            up_copy.wait_recv()

        send(even & has_up, up_copy)

        @pl.when(~even & has_down)
        def _(down_copy=down_copy):
            down_copy.wait_recv()

        send(~even & has_down, down_copy)

        @pl.when(~even & has_up)
        def _(up_copy=up_copy):
            up_copy.wait_recv()

        @pl.when(even & has_down)
        def _(down_copy=down_copy):
            down_copy.wait_recv()

    @pl.when(has_up)
    def _():
        remote(guess_down, inner.at[:, up_rows, :], a_send.at[6], a_recv.at[6], (t, s)).wait_recv()

    @pl.when(has_down)
    def _():
        remote(guess_up, inner.at[:, down_rows, :], a_send.at[7], a_recv.at[7], (t, s)).wait_recv()

    @pl.when(t > 0)
    def _():
        remote(own, inner.at[:, main_rows, :], a_send.at[8], a_recv.at[8], (t, s)).wait_recv()

    step = functools.partial(fine_step, cx=cx, cy=cy, source=source, last_strip=~has_down, blocks=blocks)

    @pl.when(t > 0)
    def _():
        def pair(i, c):
            step(u0, u1, first=TOP - 8, tiles=4)
            step(u1, u0, first=TOP - 8, tiles=4)
            return c

        lax.fori_loop(0, 2, pair, 0)

    def coarse_relaxed(b, c):
        rcx[b + 1, 0:8, :] = restrict_block(cx, b, 0, lane)
        for k in range(3):
            value = restrict_block(u0, b, 16 * k, lane)
            tcoarse[b, 8 * k : 8 * k + 8, :] = jnp.where(t > 0, value, 0.0)
        return c

    lax.fori_loop(0, cblocks, coarse_relaxed, 0)
    for r in range(0, 24, 8):
        tcoarse[cblocks, r : r + 8, :] = zero

    @pl.when(~has_down)
    def _():
        def body(b, c):
            tcoarse[b, 16:24, :] = zero
            return c

        lax.fori_loop(0, cblocks, body, 0)

    @pl.when(t < last_t)
    def _():
        step(u0, u1, first=TOP - 4, tiles=3)
        step(u1, u2, first=TOP - 4, tiles=3)
        step(u2, u1, first=TOP - 4, tiles=3)
        step(u1, u2, first=TOP, tiles=2)

        def body(b, carry):
            u, ru, turned, before = carry
            nxt = tcoarse[b + 1, 8:16, :]
            rn = pltpu.roll(nxt, L - 1, 1)
            right = jnp.where(lane == L - 1, rn, ru)
            change, turned = fluxes(
                u, right, tcoarse[b, 7:15, :], tcoarse[b, 9:17, :],
                rcx[b + 1, 8:16, :], rcx[b + 1, 7:15, :], rcy[b + 1, 8:16, :], turned, lane,
            )
            value = restrict_block(u2, b, TOP, lane) - (u + change)
            value = pltpu.roll(value, L // 2, 1)
            dwin[b, :, :] = jnp.where(lane < L // 2, before, value)
            return nxt, rn, turned, value

        u = tcoarse[0, 8:16, :]
        carry = lax.fori_loop(0, cblocks, body, (u, pltpu.roll(u, L - 1, 1), zero, zero))
        dwin[cblocks, :, :] = jnp.where(lane < L // 2, carry[3], 0.0)

    for k in range(groups):
        c = lax.rem(t + k, groups)
        piece = dwin.at[pl.ds(2 * c, 3)]
        if k == 0:
            @pl.when(t < last_t)
            def _():
                for i in range(3):
                    rd[t, i, 8:16, :] = dwin[2 * t + i, :, :]
        else:
            send(t < last_t, remote(piece, rd.at[t, :, 8:16, :], d_send.at[k, 1], d_recv.at[t, 1], (c, s)))
        send((t < last_t - 1) & has_down, remote(piece, rd.at[t, :, 0:8, :], d_send.at[k, 0], d_recv.at[t, 0], (c, s + 1)))
        send((t < last_t - 1) & has_up, remote(piece, rd.at[t, :, 16:24, :], d_send.at[k, 2], d_recv.at[t, 2], (c, s - 1)))

    @pl.when(has_up)
    def _():
        remote(wsrc, win.at[:, :, 8:16, :], w_send.at[0], w_recv.at[0], (t, s)).wait_recv()

    @pl.when(has_down)
    def _():
        remote(wsrc, win.at[:, :, 24:32, :], w_send.at[1], w_recv.at[1], (t, s)).wait_recv()

    row = lax.broadcasted_iota(jnp.int32, (8, L), 0)
    keep = {}
    for k in range(3):
        for i in range(3):
            bad = None
            if k == 2:
                bad = jnp.broadcast_to(~has_down, (8, L))
            if i == 2:
                beyond = (lane >= L // 2) & (t == last_t)
                bad = beyond if bad is None else bad | beyond
            keep[k, i] = bad
    for i in range(3):
        for k in range(3):
            fa[i, 8 + 8 * k : 16 + 8 * k, :] = win[0, i, 8 + 8 * k : 16 + 8 * k, :]
    now, later = fa, fb
    for g in range(1, groups):
        j = g - 1
        piece = dwin.at[pl.ds(0, 3)]

        @pl.when(t != j)
        def _():
            remote(piece, rd.at[j, :, 8:16, :], d_send.at[0, 1], d_recv.at[j, 1], (t, s)).wait_recv()

        if j < last_t - 1:
            @pl.when(has_up)
            def _():
                remote(piece, rd.at[j, :, 0:8, :], d_send.at[0, 0], d_recv.at[j, 0], (t, s)).wait_recv()

            @pl.when(has_down)
            def _():
                remote(piece, rd.at[j, :, 16:24, :], d_send.at[0, 2], d_recv.at[j, 2], (t, s)).wait_recv()

        middle = []
        for k in range(3):
            if j == last_t - 1 and k != 1:
                continue
            r = 8 + 8 * k
            turned = zero
            for i in range(3):
                u = now[i, r : r + 8, :]
                ru = pltpu.roll(u, L - 1, 1)
                rn = pltpu.roll(now[i + 1, r : r + 8, :], L - 1, 1) if i < 2 else zero
                right = jnp.where(lane == L - 1, rn, ru)
                change, turned = fluxes(
                    u, right, now[i, r - 1 : r + 7, :], now[i, r + 1 : r + 9, :],
                    win[1, i, r : r + 8, :], win[1, i, r - 1 : r + 7, :], win[2, i, r : r + 8, :], turned, lane,
                )
                value = u + change + rd[j, i, 8 * k : 8 * k + 8, :]
                if keep[k, i] is not None:
                    value = jnp.where(keep[k, i], 0.0, value)
                later[i, r : r + 8, :] = value
                if k == 1:
                    middle.append(pltpu.roll(value, L // 2, 1))
        for i in range(2):
            fsend[g, i, :, :] = jnp.where(lane < L // 2, middle[i], middle[i + 1])

        @pl.when(t == g)
        def _():
            for i in range(2):
                frecv[2 * t + i, :, :] = fsend[g, i, :, :]

        send(t != g, remote(fsend.at[g], frecv.at[pl.ds(2 * t, 2)], f_send.at[g], f_recv.at[t], (g, s)))
        now, later = later, now

    @pl.when(t == 0)
    def _():
        for b in range(cblocks):
            frecv[b, :, :] = inflow[b + 1, :, :]

    for c in range(groups):
        @pl.when((t > 0) & (t != c))
        def _():
            remote(fsend.at[0], frecv.at[pl.ds(2 * c, 2)], f_send.at[0], f_recv.at[c], (t, s)).wait_recv()

        for i in range(2):
            b = 2 * c + i
            error = frecv[b, :, :] - tcoarse[b, 8:16, :]
            for q in range(2):
                wide = gather_lanes(error, lane // 2 + q * (L // 2))
                f = 2 * b + q
                for p in range(2):
                    tall = jnp.take_along_axis(wide, row // 2 + 4 * p, axis=0, mode="promise_in_bounds")
                    out[8 * p : 8 * p + 8, f * L : (f + 1) * L] = tall + u0[f, TOP + 8 * p : TOP + 8 * p + 8, :]
    store = pltpu.make_async_copy(out, out_hbm.at[0], out_sem)
    store.start()
    for cond, copy in sends:
        @pl.when(cond)
        def _(copy=copy):
            copy.wait_send()
    store.wait()


def solution(mesh):
    groups, strips = mesh.shape["tm"], mesh.shape["space"]

    def shards(guesses, cond_x, cond_y, source, inflow):
        _, rows, columns = guesses.shape
        blocks = columns // L
        assert rows == 16
        cblocks = blocks // 2
        vmem = lambda *shape: pltpu.VMEM(shape, F32)
        dma = lambda *shape: pltpu.SemaphoreType.DMA(shape)
        return pl.pallas_call(
            functools.partial(kernel, groups, strips),
            out_shape=jax.ShapeDtypeStruct(guesses.shape, F32),
            in_specs=[pl.BlockSpec(memory_space=pl.ANY)] * 5,
            out_specs=pl.BlockSpec(memory_space=pl.ANY),
            scratch_shapes=[
                vmem(4, rows, columns), vmem(rows // 2, columns // 2), vmem(blocks, rows, L),
                vmem(blocks + 1, 48, L), vmem(blocks + 1, 48, L), vmem(blocks + 1, 48, L),
                vmem(blocks, 48, L), vmem(blocks, 48, L), vmem(blocks, 48, L),
                vmem(cblocks + 2, 24, L), vmem(cblocks + 2, 24, L), vmem(cblocks + 2, 8, L),
                vmem(cblocks + 1, 24, L), vmem(cblocks + 1, 8, L),
                vmem(3, 3, 8, L), vmem(3, 3, 40, L), vmem(3, 40, L), vmem(3, 40, L),
                vmem(groups - 1, 3, 24, L), vmem(groups, 2, 8, L), vmem(cblocks, 8, L), vmem(rows, columns),
                dma(5), pltpu.SemaphoreType.DMA, dma(17), dma(9), dma(2), dma(2),
                dma(groups, 3), dma(groups, 3), dma(groups), dma(groups),
            ],
            compiler_params=pltpu.CompilerParams(
                collective_id=0, has_side_effects=True, vmem_limit_bytes=40 * 2**20
            ),
        )(guesses, cond_x, cond_y, source, inflow)

    return jax.shard_map(
        shards,
        mesh=mesh,
        in_specs=(
            P("tm", "space", None),
            P("space", None),
            P("space", None),
            P("space", None),
            P("space", None),
        ),
        out_specs=P("tm", "space", None),
        check_vma=False,
    )
```

```python
import functools

import jax
import jax.numpy as jnp
from jax import lax
from jax.experimental import pallas as pl
from jax.experimental.pallas import tpu as pltpu
from jax.sharding import PartitionSpec as P

MESH = pl.DeviceIdType.MESH
F32 = jnp.float32
L = 128
TOP = 16


def remote(src, dst, send, recv, where):
    return pltpu.make_async_remote_copy(
        src_ref=src, dst_ref=dst, send_sem=send, recv_sem=recv, device_id=where, device_id_type=MESH
    )


def lane_index():
    return lax.broadcasted_iota(jnp.int32, (8, L), 1)


def gather_lanes(value, index):
    return jnp.take_along_axis(value, index, axis=1, mode="promise_in_bounds")


def restrict_block(ref, block, row, lane):
    halves = []
    for q in range(2):
        pair = ref[2 * block + q, pl.ds(row, 8, stride=2), :] + ref[
            2 * block + q, pl.ds(row + 1, 8, stride=2), :
        ]
        pair = pair + pltpu.roll(pair, L - 1, 1)
        halves.append(gather_lanes(pair, (2 * lane) % L))
    return jnp.where(lane < L // 2, halves[0], halves[1]) * 0.25


def fluxes(u, right, up, down, cx, cx_up, cy, carry, lane):
    flow = cy * (right - u)
    turned = pltpu.roll(flow, 1, 1)
    west = jnp.where(lane == 0, carry, turned)
    total = cx * (down - u) - cx_up * (u - up)
    return total + flow - west, turned


def fine_step(src, dst, cx, cy, source, first, tiles, last_strip, blocks, unroll=32):
    lane = lane_index()
    row = lax.broadcasted_iota(jnp.int32, (8, L), 0)
    rows = [first + 8 * k for k in range(tiles)]
    outside = [None if r + 8 <= TOP + 16 else (row + r >= TOP + 16) & last_strip for r in rows]

    def body(b, carry):
        new = []
        for k, r in enumerate(rows):
            u, ru, turned = carry[k]
            nxt = src[b + 1, r : r + 8, :]
            rn = pltpu.roll(nxt, L - 1, 1)
            right = jnp.where(lane == L - 1, rn, ru)
            change, turned = fluxes(
                u, right, src[b, r - 1 : r + 7, :], src[b, r + 1 : r + 9, :],
                cx[b, r : r + 8, :], cx[b, r - 1 : r + 7, :], cy[b, r : r + 8, :], turned, lane,
            )
            out = u + change + source[b, r : r + 8, :]
            if outside[k] is not None:
                out = jnp.where(outside[k], 0.0, out)
            dst[b, r : r + 8, :] = out
            new.append((nxt, rn, turned))
        return tuple(new)

    start = []
    for r in rows:
        u = src[0, r : r + 8, :]
        start.append((u, pltpu.roll(u, L - 1, 1), jnp.zeros((8, L), F32)))
    lax.fori_loop(0, blocks, body, tuple(start), unroll=unroll)


def kernel(
    groups, strips, guess_in, cx_in, cy_in, source_in, inflow_in, out_hbm,
    stage, flow_stage, own, u0, u1, u2, cx, cy, source, rcx, rcy, inflow, tcoarse, dwin,
    wsrc, win, fa, fb, rd, fsend, frecv, out,
    in_sems, out_sem, a_send, a_recv, w_send, w_recv, d_send, d_recv, f_send, f_recv,
):
    t = lax.axis_index("tm")
    s = lax.axis_index("space")
    even = lax.rem(t, 2) == 0
    has_up, has_down = s > 0, s < strips - 1
    last_t = groups - 1
    lane = lane_index()
    zero = jnp.zeros((8, L), F32)

    sends = []

    def drain():
        for cond, copy in sends:
            @pl.when(cond)
            def _(copy=copy):
                copy.wait_send()

    loads = [
        pltpu.make_async_copy(ref, stage.at[i], in_sems.at[i])
        for i, ref in enumerate((guess_in.at[0], cx_in, cy_in, source_in))
    ]
    loads.append(pltpu.make_async_copy(inflow_in, flow_stage, in_sems.at[4]))
    for load in loads:
        load.start()

    barrier = pltpu.get_barrier_semaphore()
    for k in range(1, groups):
        pl.semaphore_signal(barrier, inc=1, device_id=(lax.rem(t + k, groups), s), device_id_type=MESH)

    @pl.when(has_up)
    def _():
        for k in range(groups):
            pl.semaphore_signal(barrier, inc=1, device_id=(lax.rem(t + k, groups), s - 1), device_id_type=MESH)

    @pl.when(has_down)
    def _():
        for k in range(groups):
            pl.semaphore_signal(barrier, inc=1, device_id=(lax.rem(t + k, groups), s + 1), device_id_type=MESH)

    near = 3 - jnp.where(has_up, 0, 1) - jnp.where(has_down, 0, 1)

    for load in loads:
        load.wait()
    blocks = own.shape[0]
    cblocks = blocks // 2
    for b in range(blocks):
        cols = slice(b * L, (b + 1) * L)
        own[b, :, :] = stage[0, :, cols]
        cx[b, TOP : TOP + 16, :] = stage[1, :, cols]
        cy[b, TOP : TOP + 16, :] = stage[2, :, cols]
        source[b, TOP : TOP + 16, :] = stage[3, :, cols]
    pl.semaphore_wait(barrier, groups * near - 1)

    up_rows, down_rows, main_rows = slice(TOP - 8, TOP), slice(TOP + 16, TOP + 24), slice(TOP, TOP + 16)
    ahead = lax.rem(t + 1, groups)
    mate = jnp.where(even, t + 1, t - 1)
    coefs = (cx, cy, source)
    inner = u0.at[0:blocks]

    def send(cond, copy):
        sends.append((cond, copy))

        @pl.when(cond)
        def _():
            copy.start()

    for i, ref in enumerate(coefs):
        send(even & has_down, remote(ref.at[:, TOP + 8 : TOP + 16, :], ref.at[:, up_rows, :], a_send.at[i], a_recv.at[i], (t, s + 1)))
        send(~even & has_up, remote(ref.at[:, TOP : TOP + 8, :], ref.at[:, down_rows, :], a_send.at[3 + i], a_recv.at[3 + i], (t, s - 1)))
    guess_down, guess_up = own.at[:, 8:16, :], own.at[:, 0:8, :]
    send((t < last_t) & has_down, remote(guess_down, inner.at[:, up_rows, :], a_send.at[6], a_recv.at[6], (ahead, s + 1)))
    send((t < last_t) & has_up, remote(guess_up, inner.at[:, down_rows, :], a_send.at[7], a_recv.at[7], (ahead, s - 1)))
    send(t < last_t, remote(own, inner.at[:, main_rows, :], a_send.at[8], a_recv.at[8], (ahead, s)))
    send((t == 0) & has_down, remote(guess_down, inner.at[:, up_rows, :], a_send.at[9], a_recv.at[6], (t, s + 1)))
    send((t == 0) & has_up, remote(guess_up, inner.at[:, down_rows, :], a_send.at[10], a_recv.at[7], (t, s - 1)))

    for ref in (rcx, rcy, inflow):
        rows = ref.shape[1]
        for r in range(0, rows, 8):
            ref[0, r : r + 8, :] = zero
            ref[cblocks + 1, r : r + 8, :] = zero
    for b in range(cblocks):
        inflow[b + 1, :, :] = flow_stage[:, b * L : (b + 1) * L]

    def coarse_coefs(b, c):
        rcx[b + 1, 8:16, :] = restrict_block(cx, b, TOP, lane)
        rcy[b + 1, 8:16, :] = restrict_block(cy, b, TOP, lane)
        return c

    lax.fori_loop(0, cblocks, coarse_coefs, 0, unroll=16)

    def shifted(ref, rows):
        turned = [pltpu.roll(ref[2 * t + i, rows, :], L // 2, 1) for i in range(4)]
        return [jnp.where(lane < L // 2, turned[i], turned[i + 1]) for i in range(3)]

    for a, (ref, rows) in enumerate(((inflow, slice(0, 8)), (rcx, slice(8, 16)), (rcy, slice(8, 16)))):
        for i, value in enumerate(shifted(ref, rows)):
            wsrc[a, i, :, :] = value
            win[a, i, 16:24, :] = value
    send(has_down, remote(wsrc, win.at[:, :, 8:16, :], w_send.at[0], w_recv.at[0], (t, s + 1)))
    send(has_up, remote(wsrc, win.at[:, :, 24:32, :], w_send.at[1], w_recv.at[1], (t, s - 1)))

    def clear(ref, rows):
        def body(b, c):
            ref[b, rows, :] = zero
            return c

        lax.fori_loop(0, ref.shape[0], body, 0)

    for ref in (u0, u1, u2):
        for r in range(0, ref.shape[1], 8):
            ref[blocks, r : r + 8, :] = zero

    @pl.when(~has_up)
    def _():
        for ref in (cx, cy, source):
            clear(ref, up_rows)
        clear(inner, up_rows)
        for i in range(3):
            for a in range(3):
                win[a, i, 8:16, :] = zero
            for j in range(last_t):
                rd[j, i, 0:8, :] = zero

    @pl.when(~has_down)
    def _():
        for ref in (cx, cy, source):
            clear(ref, down_rows)
        clear(inner, down_rows)
        for i in range(3):
            for a in range(3):
                win[a, i, 24:32, :] = zero
            for j in range(last_t):
                rd[j, i, 16:24, :] = zero

    @pl.when(t == 0)
    def _():
        for b in range(blocks):
            u0[b, main_rows, :] = own[b, :, :]

    for i, ref in enumerate(coefs):
        upper, lower = ref.at[:, up_rows, :], ref.at[:, down_rows, :]
        up_copy = remote(upper, upper, a_send.at[11 + i], a_recv.at[i], (mate, s))
        down_copy = remote(lower, lower, a_send.at[14 + i], a_recv.at[3 + i], (mate, s))

        @pl.when(even & has_up)
        def _(up_copy=up_copy):
            up_copy.wait_recv()

        send(even & has_up, up_copy)

        @pl.when(~even & has_down)
        def _(down_copy=down_copy):
            down_copy.wait_recv()

        send(~even & has_down, down_copy)

        @pl.when(~even & has_up)
        def _(up_copy=up_copy):
            up_copy.wait_recv()

        @pl.when(even & has_down)
        def _(down_copy=down_copy):
            down_copy.wait_recv()

    @pl.when(has_up)
    def _():
        remote(guess_down, inner.at[:, up_rows, :], a_send.at[6], a_recv.at[6], (t, s)).wait_recv()

    @pl.when(has_down)
    def _():
        remote(guess_up, inner.at[:, down_rows, :], a_send.at[7], a_recv.at[7], (t, s)).wait_recv()

    @pl.when(t > 0)
    def _():
        remote(own, inner.at[:, main_rows, :], a_send.at[8], a_recv.at[8], (t, s)).wait_recv()

    @pl.when(has_up)
    def _():
        remote(wsrc, win.at[:, :, 8:16, :], w_send.at[0], w_recv.at[0], (t, s)).wait_recv()

    @pl.when(has_down)
    def _():
        remote(wsrc, win.at[:, :, 24:32, :], w_send.at[1], w_recv.at[1], (t, s)).wait_recv()

    step = functools.partial(fine_step, cx=cx, cy=cy, source=source, last_strip=~has_down, blocks=blocks)

    @pl.when(t > 0)
    def _():
        def pair(i, c):
            step(u0, u1, first=TOP - 8, tiles=4)
            step(u1, u0, first=TOP - 8, tiles=4)
            return c

        lax.fori_loop(0, 2, pair, 0)

    def coarse_relaxed(b, c):
        rcx[b + 1, 0:8, :] = restrict_block(cx, b, 0, lane)
        for k in range(3):
            value = restrict_block(u0, b, 16 * k, lane)
            tcoarse[b, 8 * k : 8 * k + 8, :] = jnp.where(t > 0, value, 0.0)
        return c

    lax.fori_loop(0, cblocks, coarse_relaxed, 0, unroll=16)
    for r in range(0, 24, 8):
        tcoarse[cblocks, r : r + 8, :] = zero

    @pl.when(~has_down)
    def _():
        def body(b, c):
            tcoarse[b, 16:24, :] = zero
            return c

        lax.fori_loop(0, cblocks, body, 0)

    @pl.when(t < last_t)
    def _():
        step(u0, u1, first=TOP - 4, tiles=3)
        step(u1, u2, first=TOP - 4, tiles=3)
        step(u2, u1, first=TOP - 4, tiles=3)
        step(u1, u2, first=TOP, tiles=2)

        def body(b, carry):
            u, ru, turned, before = carry
            nxt = tcoarse[b + 1, 8:16, :]
            rn = pltpu.roll(nxt, L - 1, 1)
            right = jnp.where(lane == L - 1, rn, ru)
            change, turned = fluxes(
                u, right, tcoarse[b, 7:15, :], tcoarse[b, 9:17, :],
                rcx[b + 1, 8:16, :], rcx[b + 1, 7:15, :], rcy[b + 1, 8:16, :], turned, lane,
            )
            value = restrict_block(u2, b, TOP, lane) - (u + change)
            value = pltpu.roll(value, L // 2, 1)
            dwin[b, :, :] = jnp.where(lane < L // 2, before, value)
            return nxt, rn, turned, value

        u = tcoarse[0, 8:16, :]
        carry = lax.fori_loop(0, cblocks, body, (u, pltpu.roll(u, L - 1, 1), zero, zero), unroll=16)
        dwin[cblocks, :, :] = jnp.where(lane < L // 2, carry[3], 0.0)

    for k in range(groups):
        c = lax.rem(t + k, groups)
        piece = dwin.at[pl.ds(2 * c, 3)]
        if k == 0:
            @pl.when(t < last_t)
            def _():
                for i in range(3):
                    rd[t, i, 8:16, :] = dwin[2 * t + i, :, :]
        else:
            send(t < last_t, remote(piece, rd.at[t, :, 8:16, :], d_send.at[k, 1], d_recv.at[t, 1], (c, s)))
        send((t < last_t - 1) & has_down, remote(piece, rd.at[t, :, 0:8, :], d_send.at[k, 0], d_recv.at[t, 0], (c, s + 1)))
        send((t < last_t - 1) & has_up, remote(piece, rd.at[t, :, 16:24, :], d_send.at[k, 2], d_recv.at[t, 2], (c, s - 1)))

    row = lax.broadcasted_iota(jnp.int32, (8, L), 0)
    keep = {}
    for k in range(3):
        for i in range(3):
            bad = None
            if k == 2:
                bad = jnp.broadcast_to(~has_down, (8, L))
            if i == 2:
                beyond = (lane >= L // 2) & (t == last_t)
                bad = beyond if bad is None else bad | beyond
            keep[k, i] = bad
    for i in range(3):
        for k in range(3):
            fa[i, 8 + 8 * k : 16 + 8 * k, :] = win[0, i, 8 + 8 * k : 16 + 8 * k, :]
    now, later = fa, fb
    for g in range(1, groups):
        j = g - 1
        piece = dwin.at[pl.ds(0, 3)]

        @pl.when(t != j)
        def _():
            remote(piece, rd.at[j, :, 8:16, :], d_send.at[0, 1], d_recv.at[j, 1], (t, s)).wait_recv()

        if j < last_t - 1:
            @pl.when(has_up)
            def _():
                remote(piece, rd.at[j, :, 0:8, :], d_send.at[0, 0], d_recv.at[j, 0], (t, s)).wait_recv()

            @pl.when(has_down)
            def _():
                remote(piece, rd.at[j, :, 16:24, :], d_send.at[0, 2], d_recv.at[j, 2], (t, s)).wait_recv()

        middle = []
        for k in range(3):
            if j == last_t - 1 and k != 1:
                continue
            r = 8 + 8 * k
            turned = zero
            for i in range(3):
                u = now[i, r : r + 8, :]
                ru = pltpu.roll(u, L - 1, 1)
                rn = pltpu.roll(now[i + 1, r : r + 8, :], L - 1, 1) if i < 2 else zero
                right = jnp.where(lane == L - 1, rn, ru)
                change, turned = fluxes(
                    u, right, now[i, r - 1 : r + 7, :], now[i, r + 1 : r + 9, :],
                    win[1, i, r : r + 8, :], win[1, i, r - 1 : r + 7, :], win[2, i, r : r + 8, :], turned, lane,
                )
                value = u + change + rd[j, i, 8 * k : 8 * k + 8, :]
                if keep[k, i] is not None:
                    value = jnp.where(keep[k, i], 0.0, value)
                later[i, r : r + 8, :] = value
                if k == 1:
                    middle.append(pltpu.roll(value, L // 2, 1))
        for i in range(2):
            fsend[g, i, :, :] = jnp.where(lane < L // 2, middle[i], middle[i + 1])

        @pl.when(t == g)
        def _():
            for i in range(2):
                frecv[2 * t + i, :, :] = fsend[g, i, :, :]

        send(t != g, remote(fsend.at[g], frecv.at[pl.ds(2 * t, 2)], f_send.at[g], f_recv.at[t], (g, s)))
        now, later = later, now

    @pl.when(t == 0)
    def _():
        for b in range(cblocks):
            frecv[b, :, :] = inflow[b + 1, :, :]

    for c in range(groups):
        @pl.when((t > 0) & (t != c))
        def _():
            remote(fsend.at[0], frecv.at[pl.ds(2 * c, 2)], f_send.at[0], f_recv.at[c], (t, s)).wait_recv()

        for i in range(2):
            b = 2 * c + i
            error = frecv[b, :, :] - tcoarse[b, 8:16, :]
            for q in range(2):
                wide = gather_lanes(error, lane // 2 + q * (L // 2))
                f = 2 * b + q
                for p in range(2):
                    tall = jnp.take_along_axis(wide, row // 2 + 4 * p, axis=0, mode="promise_in_bounds")
                    out[8 * p : 8 * p + 8, f * L : (f + 1) * L] = tall + u0[f, TOP + 8 * p : TOP + 8 * p + 8, :]
    store = pltpu.make_async_copy(out, out_hbm.at[0], out_sem)
    store.start()
    drain()
    store.wait()


def solution(mesh):
    groups, strips = mesh.shape["tm"], mesh.shape["space"]

    def shards(guesses, cond_x, cond_y, source, inflow):
        _, rows, columns = guesses.shape
        blocks = columns // L
        assert rows == 16
        cblocks = blocks // 2
        vmem = lambda *shape: pltpu.VMEM(shape, F32)
        dma = lambda *shape: pltpu.SemaphoreType.DMA(shape)
        return pl.pallas_call(
            functools.partial(kernel, groups, strips),
            out_shape=jax.ShapeDtypeStruct(guesses.shape, F32),
            in_specs=[pl.BlockSpec(memory_space=pl.ANY)] * 5,
            out_specs=pl.BlockSpec(memory_space=pl.ANY),
            scratch_shapes=[
                vmem(4, rows, columns), vmem(rows // 2, columns // 2), vmem(blocks, rows, L),
                vmem(blocks + 1, 48, L), vmem(blocks + 1, 48, L), vmem(blocks + 1, 48, L),
                vmem(blocks, 48, L), vmem(blocks, 48, L), vmem(blocks, 48, L),
                vmem(cblocks + 2, 24, L), vmem(cblocks + 2, 24, L), vmem(cblocks + 2, 8, L),
                vmem(cblocks + 1, 24, L), vmem(cblocks + 1, 8, L),
                vmem(3, 3, 8, L), vmem(3, 3, 40, L), vmem(3, 40, L), vmem(3, 40, L),
                vmem(groups - 1, 3, 24, L), vmem(groups, 2, 8, L), vmem(cblocks, 8, L), vmem(rows, columns),
                dma(5), pltpu.SemaphoreType.DMA, dma(17), dma(9), dma(2), dma(2),
                dma(groups, 3), dma(groups, 3), dma(groups), dma(groups),
            ],
            compiler_params=pltpu.CompilerParams(
                collective_id=0, has_side_effects=True, vmem_limit_bytes=60 * 2**20
            ),
        )(guesses, cond_x, cond_y, source, inflow)

    return jax.shard_map(
        shards,
        mesh=mesh,
        in_specs=(
            P("tm", "space", None),
            P("space", None),
            P("space", None),
            P("space", None),
            P("space", None),
        ),
        out_specs=P("tm", "space", None),
        check_vma=False,
    )
```

```python
import functools

import jax
import jax.numpy as jnp
from jax import lax
from jax.experimental import pallas as pl
from jax.experimental.pallas import tpu as pltpu
from jax.sharding import PartitionSpec as P

MESH = pl.DeviceIdType.MESH
F32 = jnp.float32
L = 128
ENDS = (10, 20, 28)
TOP = 16


def remote(src, dst, send, recv, where):
    return pltpu.make_async_remote_copy(
        src_ref=src, dst_ref=dst, send_sem=send, recv_sem=recv, device_id=where, device_id_type=MESH
    )


def lane_index():
    return lax.broadcasted_iota(jnp.int32, (8, L), 1)


def gather_lanes(value, index):
    return jnp.take_along_axis(value, index, axis=1, mode="promise_in_bounds")


def restrict_block(ref, block, row, lane):
    halves = []
    for q in range(2):
        pair = ref[2 * block + q, pl.ds(row, 8, stride=2), :] + ref[
            2 * block + q, pl.ds(row + 1, 8, stride=2), :
        ]
        pair = pair + pltpu.roll(pair, L - 1, 1)
        halves.append(gather_lanes(pair, (2 * lane) % L))
    return jnp.where(lane < L // 2, halves[0], halves[1]) * 0.25


def fluxes(u, right, up, down, cx, cx_up, cy, carry, lane):
    flow = cy * (right - u)
    turned = pltpu.roll(flow, 1, 1)
    west = jnp.where(lane == 0, carry, turned)
    total = cx * (down - u) - cx_up * (u - up)
    return total + flow - west, turned


def fine_step(src, dst, co, first, tiles, last_strip, start, stop):
    cx, cy, source = (co.at[i] for i in range(3))
    lane = lane_index()
    row = lax.broadcasted_iota(jnp.int32, (8, L), 0)
    rows = [first + 8 * k for k in range(tiles)]
    outside = [None if r + 8 <= TOP + 16 else (row + r >= TOP + 16) & last_strip for r in rows]
    state = []
    for r in rows:
        u = src[start, r : r + 8, :]
        ru = pltpu.roll(u, L - 1, 1)
        turned = jnp.zeros((8, L), F32)
        if start > 0:
            west = src[start - 1, r : r + 8, :]
            right = jnp.where(lane == L - 1, ru, pltpu.roll(west, L - 1, 1))
            turned = pltpu.roll(cy[start - 1, r : r + 8, :] * (right - west), 1, 1)
        state.append((u, ru, turned))
    for b in range(start, stop):
        for k, r in enumerate(rows):
            u, ru, turned = state[k]
            nxt = src[b + 1, r : r + 8, :]
            rn = pltpu.roll(nxt, L - 1, 1)
            right = jnp.where(lane == L - 1, rn, ru)
            change, turned = fluxes(
                u, right, src[b, r - 1 : r + 7, :], src[b, r + 1 : r + 9, :],
                cx[b, r : r + 8, :], cx[b, r - 1 : r + 7, :], cy[b, r : r + 8, :], turned, lane,
            )
            out = u + change + source[b, r : r + 8, :]
            if outside[k] is not None:
                out = jnp.where(outside[k], 0.0, out)
            dst[b, r : r + 8, :] = out
            state[k] = (nxt, rn, turned)


def kernel(
    groups, strips, guess_in, cx_in, cy_in, source_in, inflow_in, out_hbm,
    stage, flow_stage, own, u0, u1, u2, co, rcx, rcy, inflow, tcoarse, dwin,
    last_d, wsrc, win, fa, fb, rd, fsend, frecv, out,
    in_sems, out_sem, a_send, a_recv, w_send, w_recv, d_send, d_recv, f_send, f_recv,
):
    t = lax.axis_index("tm")
    s = lax.axis_index("space")
    even = lax.rem(t, 2) == 0
    has_up, has_down = s > 0, s < strips - 1
    last_t = groups - 1
    lane = lane_index()
    zero = jnp.zeros((8, L), F32)

    sends = []

    def drain():
        for cond, copy in sends:
            @pl.when(cond)
            def _(copy=copy):
                copy.wait_send()

    loads = [
        pltpu.make_async_copy(ref, stage.at[i], in_sems.at[i])
        for i, ref in enumerate((guess_in.at[0], cx_in, cy_in, source_in))
    ]
    loads.append(pltpu.make_async_copy(inflow_in, flow_stage, in_sems.at[4]))
    for load in loads:
        load.start()

    barrier = pltpu.get_barrier_semaphore()
    for k in range(1, groups):
        pl.semaphore_signal(barrier, inc=1, device_id=(lax.rem(t + k, groups), s), device_id_type=MESH)

    @pl.when(has_up)
    def _():
        for k in range(groups):
            pl.semaphore_signal(barrier, inc=1, device_id=(lax.rem(t + k, groups), s - 1), device_id_type=MESH)

    @pl.when(has_down)
    def _():
        for k in range(groups):
            pl.semaphore_signal(barrier, inc=1, device_id=(lax.rem(t + k, groups), s + 1), device_id_type=MESH)

    near = 3 - jnp.where(has_up, 0, 1) - jnp.where(has_down, 0, 1)

    for load in loads:
        load.wait()
    blocks = own.shape[0]
    cblocks = blocks // 2
    for b in range(blocks):
        cols = slice(b * L, (b + 1) * L)
        own[b, :, :] = stage[0, :, cols]
        for i in range(3):
            co[i, b, TOP : TOP + 16, :] = stage[1 + i, :, cols]
    pl.semaphore_wait(barrier, groups * near - 1)

    up_rows, down_rows, main_rows = slice(TOP - 8, TOP), slice(TOP + 16, TOP + 24), slice(TOP, TOP + 16)
    ahead = lax.rem(t + 1, groups)
    mate = jnp.where(even, t + 1, t - 1)
    inner = u0.at[0:blocks]
    ends = [e for e in ENDS if e < blocks] + [blocks]
    chunks = [slice(a, e) for a, e in zip([0] + ends[:-1], ends)]

    def send(cond, copy):
        sends.append((cond, copy))

        @pl.when(cond)
        def _():
            copy.start()

    def coef_copy(q, up, sender, where, handed=False):
        rows = up_rows if up else down_rows
        edge = slice(TOP + 8, TOP + 16) if up else slice(TOP, TOP + 8)
        there = co.at[:, chunks[q], rows, :]
        return remote(there if handed else co.at[:, chunks[q], edge, :], there, a_send.at[sender, q], a_recv.at[0 if up else 1, q], where)

    def guess_copy(q, kind, sender, where):
        rows = (slice(8, 16), slice(0, 8), slice(0, 16))[kind]
        there = (up_rows, down_rows, main_rows)[kind]
        return remote(own.at[chunks[q], rows, :], inner.at[chunks[q], there, :], a_send.at[sender, q], a_recv.at[2 + kind, q], where)

    for q in range(len(chunks)):
        send(even & has_down, coef_copy(q, True, 0, (t, s + 1)))
        send(~even & has_up, coef_copy(q, False, 0, (t, s - 1)))
        send((t < last_t) & has_down, guess_copy(q, 0, 2, (ahead, s + 1)))
        send((t < last_t) & has_up, guess_copy(q, 1, 3, (ahead, s - 1)))
        send(t < last_t, guess_copy(q, 2, 4, (ahead, s)))
        send((t == 0) & has_down, guess_copy(q, 0, 5, (t, s + 1)))
        send((t == 0) & has_up, guess_copy(q, 1, 6, (t, s - 1)))

    for ref in (rcx, rcy, inflow):
        rows = ref.shape[1]
        for r in range(0, rows, 8):
            ref[0, r : r + 8, :] = zero
            ref[cblocks + 1, r : r + 8, :] = zero
    for b in range(cblocks):
        inflow[b + 1, :, :] = flow_stage[:, b * L : (b + 1) * L]

    def coarse_coefs(b, c):
        rcx[b + 1, 8:16, :] = restrict_block(co.at[0], b, TOP, lane)
        rcy[b + 1, 8:16, :] = restrict_block(co.at[1], b, TOP, lane)
        return c

    lax.fori_loop(0, cblocks, coarse_coefs, 0, unroll=16)

    def shifted(ref, rows):
        turned = [pltpu.roll(ref[2 * t + i, rows, :], L // 2, 1) for i in range(4)]
        return [jnp.where(lane < L // 2, turned[i], turned[i + 1]) for i in range(3)]

    for a, (ref, rows) in enumerate(((inflow, slice(0, 8)), (rcx, slice(8, 16)), (rcy, slice(8, 16)))):
        for i, value in enumerate(shifted(ref, rows)):
            wsrc[a, i, :, :] = value
            win[a, i, 16:24, :] = value
    send(has_down, remote(wsrc, win.at[:, :, 8:16, :], w_send.at[0], w_recv.at[0], (t, s + 1)))
    send(has_up, remote(wsrc, win.at[:, :, 24:32, :], w_send.at[1], w_recv.at[1], (t, s - 1)))

    def clear(ref, rows):
        def body(b, c):
            ref[b, rows, :] = zero
            return c

        lax.fori_loop(0, ref.shape[0], body, 0)

    for ref in (u0, u1, u2):
        for r in range(0, ref.shape[1], 8):
            ref[blocks, r : r + 8, :] = zero

    @pl.when(~has_up)
    def _():
        for i in range(3):
            clear(co.at[i], up_rows)
        clear(inner, up_rows)
        for i in range(3):
            for a in range(3):
                win[a, i, 8:16, :] = zero
            for j in range(last_t):
                rd[j, i, 0:8, :] = zero

    @pl.when(~has_down)
    def _():
        for i in range(3):
            clear(co.at[i], down_rows)
        clear(inner, down_rows)
        for i in range(3):
            for a in range(3):
                win[a, i, 24:32, :] = zero
            for j in range(last_t):
                rd[j, i, 16:24, :] = zero

    @pl.when(t == 0)
    def _():
        for b in range(blocks):
            u0[b, main_rows, :] = own[b, :, :]

    def hand_on(q):
        up_copy = coef_copy(q, True, 1, (mate, s), handed=True)
        down_copy = coef_copy(q, False, 1, (mate, s), handed=True)

        @pl.when(even & has_up)
        def _():
            up_copy.wait_recv()

        send(even & has_up, up_copy)

        @pl.when(~even & has_down)
        def _():
            down_copy.wait_recv()

        send(~even & has_down, down_copy)

    def arrive(q):
        @pl.when(~even & has_up)
        def _():
            coef_copy(q, True, 1, (mate, s), handed=True).wait_recv()

        @pl.when(even & has_down)
        def _():
            coef_copy(q, False, 1, (mate, s), handed=True).wait_recv()

        @pl.when(has_up)
        def _():
            guess_copy(q, 0, 2, (t, s)).wait_recv()

        @pl.when(has_down)
        def _():
            guess_copy(q, 1, 3, (t, s)).wait_recv()

        @pl.when(t > 0)
        def _():
            guess_copy(q, 2, 4, (t, s)).wait_recv()

    plan = [
        (u0, u1, -8, 4), (u1, u0, -8, 4), (u0, u1, -8, 4), (u1, u0, -4, 3),
        (u0, u1, -4, 3), (u1, u2, -4, 3), (u2, u1, -4, 3), (u1, u2, 0, 2),
    ]

    def ready(end, lag):
        return blocks if end == blocks else max(0, end - lag)

    def steps(levels, before, end):
        for level in levels:
            src, dst, first, tiles = plan[level - 1]
            start, stop = ready(before, level) if before else 0, ready(end, level)
            if start < stop:
                fine_step(src, dst, co, TOP + first, tiles, ~has_down, start, stop)

    def coarse_relaxed(start, stop):
        for b in range(start, stop):
            rcx[b + 1, 0:8, :] = restrict_block(co.at[0], b, 0, lane)
            for k in range(3):
                value = restrict_block(u0, b, 16 * k, lane)
                drop = t == 0
                if k == 2:
                    drop = drop | ~has_down
                tcoarse[b, 8 * k : 8 * k + 8, :] = jnp.where(drop, 0.0, value)

    def differences(start, stop):
        u = tcoarse[start, 8:16, :]
        ru = pltpu.roll(u, L - 1, 1)
        turned = before = zero
        if start > 0:
            west = tcoarse[start - 1, 8:16, :]
            right = jnp.where(lane == L - 1, ru, pltpu.roll(west, L - 1, 1))
            turned = pltpu.roll(rcy[start, 8:16, :] * (right - west), 1, 1)
            before = last_d[...]
        for b in range(start, stop):
            nxt = tcoarse[b + 1, 8:16, :]
            rn = pltpu.roll(nxt, L - 1, 1)
            right = jnp.where(lane == L - 1, rn, ru)
            change, turned = fluxes(
                u, right, tcoarse[b, 7:15, :], tcoarse[b, 9:17, :],
                rcx[b + 1, 8:16, :], rcx[b + 1, 7:15, :], rcy[b + 1, 8:16, :], turned, lane,
            )
            value = restrict_block(u2, b, TOP, lane) - (u + change)
            value = pltpu.roll(value, L // 2, 1)
            dwin[b, :, :] = jnp.where(lane < L // 2, before, value)
            u, ru, before = nxt, rn, value
        last_d[...] = before
        if stop == cblocks:
            dwin[cblocks, :, :] = jnp.where(lane < L // 2, before, 0.0)

    def halo_rows(j):
        return 2 * ((last_t - j) // 2)

    def window_copy(c, j, part, where):
        halo = halo_rows(j)
        mine = (slice(8 - halo, 8), slice(0, 8), slice(0, halo))[part]
        there = (slice(8 - halo, 8), slice(8, 16), slice(16, 16 + halo))[part]
        return remote(
            dwin.at[pl.ds(2 * c, 3), mine, :], rd.at[t if where else j, :, there, :],
            d_send.at[c, part], d_recv.at[t if where else j, part], where or (t, s),
        )

    def windows(start, stop):
        for k in range(stop - start):
            c = start + lax.rem(t + k, stop - start)

            @pl.when((c == t) & (t < last_t))
            def _():
                for i in range(3):
                    rd[t, i, 8:16, :] = dwin[2 * t + i, :, :]

            send((c != t) & (t < last_t), window_copy(c, 0, 1, (c, s)))
            for j in range(0, last_t - 1, 2):
                among = (t >= j) & (t < j + 2)
                send(among & has_down, window_copy(c, j + 1, 0, (c, s + 1)))
                send(among & has_up, window_copy(c, j + 1, 2, (c, s - 1)))

    for r in range(0, 24, 8):
        tcoarse[cblocks, r : r + 8, :] = zero
    hand_on(0)
    end = t_done = d_done = w_done = 0
    for q in range(len(chunks)):
        if q + 1 < len(chunks):
            hand_on(q + 1)
        arrive(q)
        before, end = end, ends[q]
        t_from, t_done = t_done, ready(end, 4) // 2
        d_from, d_done = d_done, ready(end, 8) // 2
        w_from, w_done = w_done, groups if end == blocks else max(0, (d_done - 1) // 2)

        @pl.when(t > 0)
        def _():
            steps((1, 2, 3, 4), before, end)

        coarse_relaxed(t_from, t_done)

        @pl.when(t < last_t)
        def _():
            steps((5, 6, 7, 8), before, end)
            if d_from < d_done:
                differences(d_from, d_done)

        if w_from < w_done:
            windows(w_from, w_done)

    @pl.when(has_up)
    def _():
        remote(wsrc, win.at[:, :, 8:16, :], w_send.at[0], w_recv.at[0], (t, s)).wait_recv()

    @pl.when(has_down)
    def _():
        remote(wsrc, win.at[:, :, 24:32, :], w_send.at[1], w_recv.at[1], (t, s)).wait_recv()

    row = lax.broadcasted_iota(jnp.int32, (8, L), 0)
    keep = {}
    for k in range(3):
        for i in range(3):
            bad = None
            if k == 2:
                bad = jnp.broadcast_to(~has_down, (8, L))
            if i == 2:
                beyond = (lane >= L // 2) & (t == last_t)
                bad = beyond if bad is None else bad | beyond
            keep[k, i] = bad
    for i in range(3):
        for k in range(3):
            fa[i, 8 + 8 * k : 16 + 8 * k, :] = win[0, i, 8 + 8 * k : 16 + 8 * k, :]
    now, later = fa, fb
    for g in range(1, groups):
        j = g - 1

        @pl.when(t != j)
        def _():
            window_copy(0, j, 1, None).wait_recv()

        if j < last_t - 1:
            @pl.when(has_up)
            def _():
                window_copy(0, j, 0, None).wait_recv()

            @pl.when(has_down)
            def _():
                window_copy(0, j, 2, None).wait_recv()

        middle = []
        for k in range(3):
            if j == last_t - 1 and k != 1:
                continue
            r = 8 + 8 * k
            turned = zero
            for i in range(3):
                u = now[i, r : r + 8, :]
                ru = pltpu.roll(u, L - 1, 1)
                rn = pltpu.roll(now[i + 1, r : r + 8, :], L - 1, 1) if i < 2 else zero
                right = jnp.where(lane == L - 1, rn, ru)
                change, turned = fluxes(
                    u, right, now[i, r - 1 : r + 7, :], now[i, r + 1 : r + 9, :],
                    win[1, i, r : r + 8, :], win[1, i, r - 1 : r + 7, :], win[2, i, r : r + 8, :], turned, lane,
                )
                value = u + change + rd[j, i, 8 * k : 8 * k + 8, :]
                if keep[k, i] is not None:
                    value = jnp.where(keep[k, i], 0.0, value)
                later[i, r : r + 8, :] = value
                if k == 1:
                    middle.append(pltpu.roll(value, L // 2, 1))
        for i in range(2):
            fsend[g, i, :, :] = jnp.where(lane < L // 2, middle[i], middle[i + 1])

        @pl.when(t == g)
        def _():
            for i in range(2):
                frecv[2 * t + i, :, :] = fsend[g, i, :, :]

        send(t != g, remote(fsend.at[g], frecv.at[pl.ds(2 * t, 2)], f_send.at[g], f_recv.at[t], (g, s)))
        now, later = later, now

    @pl.when(t == 0)
    def _():
        for b in range(cblocks):
            frecv[b, :, :] = inflow[b + 1, :, :]

    for c in range(groups):
        @pl.when((t > 0) & (t != c))
        def _():
            remote(fsend.at[0], frecv.at[pl.ds(2 * c, 2)], f_send.at[0], f_recv.at[c], (t, s)).wait_recv()

        for i in range(2):
            b = 2 * c + i
            error = frecv[b, :, :] - tcoarse[b, 8:16, :]
            for q in range(2):
                wide = gather_lanes(error, lane // 2 + q * (L // 2))
                f = 2 * b + q
                for p in range(2):
                    tall = jnp.take_along_axis(wide, row // 2 + 4 * p, axis=0, mode="promise_in_bounds")
                    out[8 * p : 8 * p + 8, f * L : (f + 1) * L] = tall + u0[f, TOP + 8 * p : TOP + 8 * p + 8, :]
    store = pltpu.make_async_copy(out, out_hbm.at[0], out_sem)
    store.start()
    drain()
    store.wait()


def solution(mesh):
    groups, strips = mesh.shape["tm"], mesh.shape["space"]

    def shards(guesses, cond_x, cond_y, source, inflow):
        _, rows, columns = guesses.shape
        blocks = columns // L
        assert rows == 16
        cblocks = blocks // 2
        vmem = lambda *shape: pltpu.VMEM(shape, F32)
        dma = lambda *shape: pltpu.SemaphoreType.DMA(shape)
        return pl.pallas_call(
            functools.partial(kernel, groups, strips),
            out_shape=jax.ShapeDtypeStruct(guesses.shape, F32),
            in_specs=[pl.BlockSpec(memory_space=pl.ANY)] * 5,
            out_specs=pl.BlockSpec(memory_space=pl.ANY),
            scratch_shapes=[
                vmem(4, rows, columns), vmem(rows // 2, columns // 2), vmem(blocks, rows, L),
                vmem(blocks + 1, 48, L), vmem(blocks + 1, 48, L), vmem(blocks + 1, 48, L),
                vmem(3, blocks, 48, L),
                vmem(cblocks + 2, 24, L), vmem(cblocks + 2, 24, L), vmem(cblocks + 2, 8, L),
                vmem(cblocks + 1, 24, L), vmem(cblocks + 1, 8, L),
                vmem(8, L), vmem(3, 3, 8, L), vmem(3, 3, 40, L), vmem(3, 40, L), vmem(3, 40, L),
                vmem(groups - 1, 3, 24, L), vmem(groups, 2, 8, L), vmem(cblocks, 8, L), vmem(rows, columns),
                dma(5), pltpu.SemaphoreType.DMA, dma(7, 8), dma(5, 8), dma(2), dma(2),
                dma(groups, 3), dma(groups, 3), dma(groups), dma(groups),
            ],
            compiler_params=pltpu.CompilerParams(
                collective_id=0, has_side_effects=True, vmem_limit_bytes=60 * 2**20
            ),
        )(guesses, cond_x, cond_y, source, inflow)

    return jax.shard_map(
        shards,
        mesh=mesh,
        in_specs=(
            P("tm", "space", None),
            P("space", None),
            P("space", None),
            P("space", None),
            P("space", None),
        ),
        out_specs=P("tm", "space", None),
        check_vma=False,
    )
```

```python
import functools

import jax
import jax.numpy as jnp
from jax import lax
from jax.experimental import pallas as pl
from jax.experimental.pallas import tpu as pltpu
from jax.sharding import PartitionSpec as P

MESH = pl.DeviceIdType.MESH
F32 = jnp.float32
L = 128
H = L // 2
TOP = 16
UP, DOWN, MAIN = slice(TOP - 8, TOP), slice(TOP + 16, TOP + 24), slice(TOP, TOP + 16)
PAIRS = ((0, 1), (7, 6), (2, 3), (5, 4))


def remote(src, dst, send, recv, where):
    return pltpu.make_async_remote_copy(
        src_ref=src, dst_ref=dst, send_sem=send, recv_sem=recv, device_id=where, device_id_type=MESH
    )


def gather(value, index, axis):
    return jnp.take_along_axis(value, index, axis=axis, mode="promise_in_bounds")


def restrict_block(ref, block, row, lane):
    halves = []
    for q in range(2):
        if 2 * block + q >= ref.shape[0]:
            halves.append(jnp.zeros((8, L), F32))
            continue
        pair = ref[2 * block + q, pl.ds(row, 8, stride=2), :] + ref[
            2 * block + q, pl.ds(row + 1, 8, stride=2), :
        ]
        pair = pair + pltpu.roll(pair, L - 1, 1)
        halves.append(gather(pair, (2 * lane) % L, 1))
    return jnp.where(lane < H, halves[0], halves[1]) * 0.25


def fluxes(u, right, up, down, cx, cx_up, cy, carry, lane):
    flow = cy * (right - u)
    turned = pltpu.roll(flow, 1, 1)
    west = jnp.where(lane == 0, carry, turned)
    total = cx * (down - u) - cx_up * (u - up)
    return total + flow - west, turned


def fine_step(pairs, co, first, tiles, last_strip, last_window):
    cx, cy, source = (co.at[i] for i in range(3))
    blocks = co.shape[1]
    lane = lax.broadcasted_iota(jnp.int32, (8, L), 1)
    row = lax.broadcasted_iota(jnp.int32, (8, L), 0)
    zero = jnp.zeros((8, L), F32)
    rows = [first + 8 * k for k in range(tiles)]
    below = [None if r + 8 <= TOP + 16 else (row + r >= TOP + 16) & last_strip for r in rows]
    beyond = (lane >= H) & last_window
    state = {}
    for n, (src, _) in enumerate(pairs):
        for k, r in enumerate(rows):
            u = src[0, r : r + 8, :]
            state[n, k] = (u, pltpu.roll(u, L - 1, 1), zero)
    for b in range(blocks):
        for n, (src, dst) in enumerate(pairs):
            for k, r in enumerate(rows):
                u, ru, turned = state[n, k]
                nxt, rn = zero, zero
                if b + 1 < blocks:
                    nxt = src[b + 1, r : r + 8, :]
                    rn = pltpu.roll(nxt, L - 1, 1)
                right = jnp.where(lane == L - 1, rn, ru)
                change, turned = fluxes(
                    u, right, src[b, r - 1 : r + 7, :], src[b, r + 1 : r + 9, :],
                    cx[b, r : r + 8, :], cx[b, r - 1 : r + 7, :], cy[b, r : r + 8, :], turned, lane,
                )
                out = u + change + source[b, r : r + 8, :]
                drop = below[k]
                if b + 1 == blocks:
                    drop = beyond if drop is None else drop | beyond
                if drop is not None:
                    out = jnp.where(drop, 0.0, out)
                dst[b, r : r + 8, :] = out
                state[n, k] = (nxt, rn, turned)


def kernel(
    groups, strips, guess_in, cx_in, cy_in, source_in, inflow_in, out_hbm,
    stage, flow_stage, shifted, guess, relaxed, ua, ub, co, tcoarse, wsrc, win, rd, fa, fb, outw,
    in_sems, g_send, g_recv, c_send, c_recv, w_send, w_recv, d_send, d_recv, o_send, o_recv, own_sem,
):
    t = lax.axis_index("tm")
    s = lax.axis_index("space")
    has_up, has_down = s > 0, s < strips - 1
    last = groups - 1
    lane = lax.broadcasted_iota(jnp.int32, (8, L), 1)
    row = lax.broadcasted_iota(jnp.int32, (8, L), 0)
    zero = jnp.zeros((8, L), F32)
    blocks = shifted.shape[0] - 1
    width = blocks // groups
    cwidth = width // 2
    wb = width + 1
    sends = []

    def send(cond, copy):
        sends.append((cond, copy))

        @pl.when(cond)
        def _():
            copy.start()

    def drain():
        for cond, copy in sends:
            @pl.when(cond)
            def _(copy=copy):
                copy.wait_send()

    loads = [
        pltpu.make_async_copy(ref, stage.at[i], in_sems.at[i])
        for i, ref in enumerate((guess_in.at[0], cx_in, cy_in, source_in))
    ]
    loads.append(pltpu.make_async_copy(inflow_in, flow_stage, in_sems.at[4]))
    for load in loads:
        load.start()

    barrier = pltpu.get_barrier_semaphore()
    for k in range(1, groups):
        pl.semaphore_signal(barrier, inc=1, device_id=(lax.rem(t + k, groups), s), device_id_type=MESH)

    @pl.when(has_up)
    def _():
        for k in range(groups):
            pl.semaphore_signal(barrier, inc=1, device_id=(lax.rem(t + k, groups), s - 1), device_id_type=MESH)

    @pl.when(has_down)
    def _():
        for k in range(groups):
            pl.semaphore_signal(barrier, inc=1, device_id=(lax.rem(t + k, groups), s + 1), device_id_type=MESH)

    near = 3 - jnp.where(has_up, 0, 1) - jnp.where(has_down, 0, 1)

    for load in loads:
        load.wait()
    for r in range(0, 16, 8):
        before = zero
        for b in range(blocks):
            turned = pltpu.roll(stage[0, r : r + 8, b * L : (b + 1) * L], H, 1)
            shifted[b, r : r + 8, :] = jnp.where(lane < H, before, turned)
            before = turned
        shifted[blocks, r : r + 8, :] = jnp.where(lane < H, before, 0.0)

    def around(ref, a, rows, count, per):
        values = []
        for n in range(-1, count + 1):
            at = jnp.clip(t * per + n, 0, per * groups - 1)
            cols = pl.ds(pl.multiple_of(at * L, L), L)
            value = ref[rows, cols] if a is None else ref[a, rows, cols]
            if n < 0:
                value = jnp.where(t == 0, 0.0, value)
            if n == count:
                value = jnp.where(t == last, 0.0, value)
            values.append(value)
        return values

    for a in range(3):
        for r in range(0, 16, 8):
            turned = [pltpu.roll(v, H, 1) for v in around(stage, 1 + a, slice(r, r + 8), width, width)]
            for i in range(wb):
                co[a, i, TOP + r : TOP + r + 8, :] = jnp.where(lane < H, turned[i], turned[i + 1])
    pl.semaphore_wait(barrier, groups * near - 1)

    def guess_copy(k, part, where):
        c = lax.rem(t - k + groups, groups)
        mine = (slice(0, 16), slice(8, 16), slice(0, 8))[part]
        there = (MAIN, UP, DOWN)[part]
        return remote(
            shifted.at[pl.ds(width * c, wb), mine, :], guess.at[k, :, there, :],
            g_send.at[part, k], g_recv.at[part, k], where or (c, s + (0, 1, -1)[part]),
        )

    send(has_down, remote(co.at[:, :, TOP + 8 : TOP + 16, :], co.at[:, :, UP, :], c_send.at[0], c_recv.at[0], (t, s + 1)))
    send(has_up, remote(co.at[:, :, TOP : TOP + 8, :], co.at[:, :, DOWN, :], c_send.at[1], c_recv.at[1], (t, s - 1)))
    for k in [k for pair in PAIRS for k in pair]:
        send((t < last) & has_down, guess_copy(k, 1, None))
        send((t < last) & has_up, guess_copy(k, 2, None))
        if k > 0:
            send(t < last, guess_copy(k, 0, None))

    turned = [pltpu.roll(v, H // 2, 1) for v in around(flow_stage, None, slice(0, 8), cwidth, cwidth)]
    for i in range(cwidth + 1):
        value = jnp.where(lane < H // 2, turned[i], turned[i + 1])
        for a in range(3):
            if a > 0:
                value = restrict_block(co.at[a - 1], i, TOP, lane)
            wsrc[a, i, :, :] = value
            win[a, i, 16:24, :] = value
    w_down = remote(wsrc, win.at[:, :, 8:16, :], w_send.at[0], w_recv.at[0], (t, s + 1))
    w_up = remote(wsrc, win.at[:, :, 24:32, :], w_send.at[1], w_recv.at[1], (t, s - 1))
    send(has_down, w_down)
    send(has_up, w_up)

    def clear(fine, coarse, halo):
        for i in range(wb):
            for a in range(3):
                co[a, i, fine, :] = zero
            for k in range(groups):
                guess[k, i, fine, :] = zero
        for i in range(cwidth + 1):
            for a in range(3):
                win[a, i, coarse, :] = zero
            for j in range(groups):
                rd[j, i, halo, :] = zero

    @pl.when(~has_up)
    def _():
        clear(UP, slice(8, 16), slice(0, 8))

    @pl.when(~has_down)
    def _():
        clear(DOWN, slice(24, 32), slice(16, 24))

    for i in range(wb):
        guess[0, i, MAIN, :] = shifted[width * t + i, :, :]

    @pl.when(has_up)
    def _():
        remote(co.at[:, :, TOP + 8 : TOP + 16, :], co.at[:, :, UP, :], c_send.at[0], c_recv.at[0], (t, s)).wait_recv()
        remote(wsrc, win.at[:, :, 8:16, :], w_send.at[0], w_recv.at[0], (t, s)).wait_recv()

    @pl.when(has_down)
    def _():
        remote(co.at[:, :, TOP : TOP + 8, :], co.at[:, :, DOWN, :], c_send.at[1], c_recv.at[1], (t, s)).wait_recv()
        remote(wsrc, win.at[:, :, 24:32, :], w_send.at[1], w_recv.at[1], (t, s)).wait_recv()

    def arrive(k):
        held = lax.rem(t + k, groups) < last

        @pl.when(held & has_up)
        def _():
            guess_copy(k, 1, (t, s)).wait_recv()

        @pl.when(held & has_down)
        def _():
            guess_copy(k, 2, (t, s)).wait_recv()

        if k > 0:
            @pl.when(held)
            def _():
                guess_copy(k, 0, (t, s)).wait_recv()

    step = functools.partial(fine_step, co=co, last_strip=~has_down, last_window=t == last)
    for pair in PAIRS:
        for k in pair:
            arrive(k)
        g0, r0 = [guess.at[k] for k in pair], [relaxed.at[k] for k in pair]
        a0, b0 = [ua.at[n] for n in range(2)], [ub.at[n] for n in range(2)]
        for src, dst, first, tiles in (
            (g0, a0, -8, 4), (a0, b0, -8, 4), (b0, a0, -8, 4), (a0, r0, -4, 3),
            (r0, a0, -4, 3), (a0, b0, -4, 3), (b0, a0, -4, 3), (a0, b0, 0, 2),
        ):
            step(list(zip(src, dst)), first=TOP + first, tiles=tiles)
        for n, k in enumerate(pair):
            o = lax.rem(t + k, groups) + 1
            for i in range(cwidth + 1):
                for m in range(3):
                    value = restrict_block(relaxed.at[k], i, 16 * m, lane)
                    if m == 2:
                        value = jnp.where(has_down, value, 0.0)
                    tcoarse[o, i, 8 * m : 8 * m + 8, :] = value
        for n, k in enumerate(pair):
            o = lax.rem(t + k, groups) + 1
            turned = zero
            for i in range(cwidth + 1):
                u = tcoarse[o, i, 8:16, :]
                rn = pltpu.roll(tcoarse[o, i + 1, 8:16, :], L - 1, 1) if i < cwidth else zero
                right = jnp.where(lane == L - 1, rn, pltpu.roll(u, L - 1, 1))
                change, turned = fluxes(
                    u, right, tcoarse[o, i, 7:15, :], tcoarse[o, i, 9:17, :],
                    win[1, i, 16:24, :], win[1, i, 15:23, :], win[2, i, 16:24, :], turned, lane,
                )
                rd[o, i, 8:16, :] = restrict_block(ub.at[n], i, TOP, lane) - (u + change)
    for i in range(cwidth + 1):
        rd[0, i, 8:16, :] = tcoarse[1, i, 8:16, :]

    def d_copy(j, part, where):
        halo = last - 1 - j
        mine = (slice(16 - halo, 16), slice(8, 8 + halo))[part]
        there = (slice(8 - halo, 8), slice(16, 16 + halo))[part]
        both = slice(j, j + 2)
        return remote(rd.at[both, :, mine, :], rd.at[both, :, there, :], d_send.at[part, j], d_recv.at[part, j], where)

    for j in range(0, last - 1, 2):
        send(has_down, d_copy(j, 0, (t, s + 1)))
        send(has_up, d_copy(j, 1, (t, s - 1)))

    for g in range(groups):
        k = lax.rem(g - 1 - t + 2 * groups, groups) if g > 0 else lax.rem(groups - t, groups)
        ref = relaxed if g > 0 else guess
        for r in range(0, 16, 8):
            turned = [pltpu.roll(ref[k, i, TOP + r : TOP + r + 8, :], H, 1) for i in range(wb)]
            for i in range(width):
                outw[g, r : r + 8, i * L : (i + 1) * L] = jnp.where(lane < H, turned[i], turned[i + 1])

    def finish(g, error):
        for i in range(width):
            base = H // 2 + H * i
            at = base % L + lane // 2
            wide = gather(error[base // L], at % L, 1)
            if base % L + H > L:
                wide = jnp.where(at < L, wide, gather(error[base // L + 1], at % L, 1))
            for p in range(2):
                tall = gather(wide, row // 2 + 4 * p, 0)
                rows, cols = slice(8 * p, 8 * p + 8), slice(i * L, (i + 1) * L)
                outw[g, rows, cols] = outw[g, rows, cols] + tall
        send(t != g, out_copy(g, t, (g, s)))

        @pl.when(t == g)
        def _():
            own_copy(g).start()

    def out_copy(g, c, where):
        cols = pl.ds(pl.multiple_of(c * (width * L), L), width * L)
        return remote(outw.at[g], out_hbm.at[0, :, cols], o_send.at[g], o_recv.at[c], where)

    def own_copy(g):
        cols = pl.ds(pl.multiple_of(t * (width * L), L), width * L)
        return pltpu.make_async_copy(outw.at[g], out_hbm.at[0, :, cols], own_sem)

    finish(0, [win[0, i, 16:24, :] for i in range(cwidth + 1)])

    keep = {}
    for k in range(3):
        for i in range(cwidth + 1):
            bad = jnp.broadcast_to(~has_down, (8, L)) if k == 2 else None
            if i == cwidth:
                beyond = (lane >= H // 2) & (t == last)
                bad = beyond if bad is None else bad | beyond
            keep[k, i] = bad
    now, later = win.at[0], fa
    for g in range(1, groups):
        j = g - 1
        if j % 2 == 0 and j < last - 1:
            @pl.when(has_up)
            def _():
                d_copy(j, 0, (t, s)).wait_recv()

            @pl.when(has_down)
            def _():
                d_copy(j, 1, (t, s)).wait_recv()

        error = []
        for k in range(3):
            if g == last and k != 1:
                continue
            r = 8 + 8 * k
            turned = zero
            for i in range(cwidth + 1):
                u = now[i, r : r + 8, :]
                rn = pltpu.roll(now[i + 1, r : r + 8, :], L - 1, 1) if i < cwidth else zero
                right = jnp.where(lane == L - 1, rn, pltpu.roll(u, L - 1, 1))
                change, turned = fluxes(
                    u, right, now[i, r - 1 : r + 7, :], now[i, r + 1 : r + 9, :],
                    win[1, i, r : r + 8, :], win[1, i, r - 1 : r + 7, :], win[2, i, r : r + 8, :], turned, lane,
                )
                value = u + change + rd[j, i, 8 * k : 8 * k + 8, :]
                if keep[k, i] is not None:
                    value = jnp.where(keep[k, i], 0.0, value)
                if g < last:
                    later[i, r : r + 8, :] = value
                if k == 1:
                    error.append(value - tcoarse[g, i, 8:16, :])
        now, later = later, (fb if later is fa else fa)
        finish(g, error)

    for c in range(groups):
        @pl.when(t != c)
        def _():
            out_copy(0, c, (t, s)).wait_recv()

    drain()
    own_copy(0).wait()


def solution(mesh):
    groups, strips = mesh.shape["tm"], mesh.shape["space"]

    def shards(guesses, cond_x, cond_y, source, inflow):
        _, rows, columns = guesses.shape
        blocks = columns // L
        assert rows == 16 and groups == 8 and blocks == 4 * groups
        vmem = lambda *shape: pltpu.VMEM(shape, F32)
        dma = lambda *shape: pltpu.SemaphoreType.DMA(shape)
        return pl.pallas_call(
            functools.partial(kernel, groups, strips),
            out_shape=jax.ShapeDtypeStruct(guesses.shape, F32),
            in_specs=[pl.BlockSpec(memory_space=pl.ANY)] * 5,
            out_specs=pl.BlockSpec(memory_space=pl.ANY),
            scratch_shapes=[
                vmem(4, rows, columns), vmem(rows // 2, columns // 2), vmem(blocks + 1, rows, L),
                vmem(groups, 5, 48, L), vmem(groups, 5, 48, L), vmem(2, 5, 48, L), vmem(2, 5, 48, L),
                vmem(3, 5, 48, L), vmem(groups + 1, 3, 24, L), vmem(3, 3, 8, L), vmem(3, 3, 40, L),
                vmem(groups + 1, 3, 24, L), vmem(3, 40, L), vmem(3, 40, L), vmem(groups, rows, 4 * L),
                dma(5), dma(3, groups), dma(3, groups), dma(2), dma(2), dma(2), dma(2),
                dma(2, groups), dma(2, groups), dma(groups), dma(groups), pltpu.SemaphoreType.DMA,
            ],
            compiler_params=pltpu.CompilerParams(
                collective_id=0, has_side_effects=True, vmem_limit_bytes=60 * 2**20
            ),
        )(guesses, cond_x, cond_y, source, inflow)

    return jax.shard_map(
        shards,
        mesh=mesh,
        in_specs=(
            P("tm", "space", None),
            P("space", None),
            P("space", None),
            P("space", None),
            P("space", None),
        ),
        out_specs=P("tm", "space", None),
        check_vma=False,
    )
```

```python
import functools

import jax
import jax.numpy as jnp
from jax import lax
from jax.experimental import pallas as pl
from jax.experimental.pallas import tpu as pltpu
from jax.sharding import PartitionSpec as P

MESH = pl.DeviceIdType.MESH
F32 = jnp.float32
L = 128
H = L // 2
TOP = 16
UP, DOWN, MAIN = slice(TOP - 8, TOP), slice(TOP + 16, TOP + 24), slice(TOP, TOP + 16)
ROUNDS = ((0, 1, 7, 2), (3, 4, 5, 6))
SPLIT = False
BATCHES = (2, 4, 6, 7)


def remote(src, dst, send, recv, where):
    return pltpu.make_async_remote_copy(
        src_ref=src, dst_ref=dst, send_sem=send, recv_sem=recv, device_id=where, device_id_type=MESH
    )


def gather(value, index, axis):
    return jnp.take_along_axis(value, index, axis=axis, mode="promise_in_bounds")


def restrict_block(ref, block, row, lane):
    halves = []
    for q in range(2):
        if 2 * block + q >= ref.shape[0]:
            halves.append(jnp.zeros((8, L), F32))
            continue
        pair = ref[2 * block + q, pl.ds(row, 8, stride=2), :] + ref[
            2 * block + q, pl.ds(row + 1, 8, stride=2), :
        ]
        pair = pair + pltpu.roll(pair, L - 1, 1)
        halves.append(gather(pair, (2 * lane) % L, 1))
    return jnp.where(lane < H, halves[0], halves[1]) * 0.25


def fluxes(u, right, up, down, cx, cx_up, cy, carry, lane):
    flow = cy * (right - u)
    turned = pltpu.roll(flow, 1, 1)
    west = jnp.where(lane == 0, carry, turned)
    total = cx * (down - u) - cx_up * (u - up)
    return total + flow - west, turned


def fine_step(pairs, co, first, tiles, last_strip, last_window):
    cx, cy, source = (co.at[i] for i in range(3))
    blocks = co.shape[1]
    lane = lax.broadcasted_iota(jnp.int32, (8, L), 1)
    row = lax.broadcasted_iota(jnp.int32, (8, L), 0)
    zero = jnp.zeros((8, L), F32)
    rows = [first + 8 * k for k in range(tiles)]
    below = [None if r + 8 <= TOP + 16 else (row + r >= TOP + 16) & last_strip for r in rows]
    beyond = (lane >= H) & last_window
    state = {}
    for n, (src, _) in enumerate(pairs):
        for k, r in enumerate(rows):
            u = src[0, r : r + 8, :]
            state[n, k] = (u, pltpu.roll(u, L - 1, 1), zero)
    for b in range(blocks):
        for n, (src, dst) in enumerate(pairs):
            for k, r in enumerate(rows):
                u, ru, turned = state[n, k]
                nxt, rn = zero, zero
                if b + 1 < blocks:
                    nxt = src[b + 1, r : r + 8, :]
                    rn = pltpu.roll(nxt, L - 1, 1)
                right = jnp.where(lane == L - 1, rn, ru)
                change, turned = fluxes(
                    u, right, src[b, r - 1 : r + 7, :], src[b, r + 1 : r + 9, :],
                    cx[b, r : r + 8, :], cx[b, r - 1 : r + 7, :], cy[b, r : r + 8, :], turned, lane,
                )
                out = u + change + source[b, r : r + 8, :]
                drop = below[k]
                if b + 1 == blocks:
                    drop = beyond if drop is None else drop | beyond
                if drop is not None:
                    out = jnp.where(drop, 0.0, out)
                dst[b, r : r + 8, :] = out
                state[n, k] = (nxt, rn, turned)


def kernel(
    groups, strips, guess_in, cx_in, cy_in, source_in, inflow_in, out_hbm,
    stage, flow_stage, shifted, guess, relaxed, ua, ub, co, tcoarse, wsrc, win, rd, fa, fb, outw,
    in_sems, g_send, g_recv, c_send, c_recv, w_send, w_recv, d_send, d_recv, o_send, o_recv, own_sem,
):
    t = lax.axis_index("tm")
    s = lax.axis_index("space")
    has_up, has_down = s > 0, s < strips - 1
    last = groups - 1
    lane = lax.broadcasted_iota(jnp.int32, (8, L), 1)
    row = lax.broadcasted_iota(jnp.int32, (8, L), 0)
    zero = jnp.zeros((8, L), F32)
    blocks = shifted.shape[0] - 1
    width = blocks // groups
    cwidth = width // 2
    wb = width + 1
    sends = []

    def send(cond, copy):
        sends.append((cond, copy))

        @pl.when(cond)
        def _():
            copy.start()

    def drain():
        for cond, copy in sends:
            @pl.when(cond)
            def _(copy=copy):
                copy.wait_send()
        sends.clear()

    loads = [
        pltpu.make_async_copy(ref, stage.at[i], in_sems.at[i])
        for i, ref in enumerate((guess_in.at[0], cx_in, cy_in, source_in))
    ]
    loads.append(pltpu.make_async_copy(inflow_in, flow_stage, in_sems.at[4]))
    for load in loads:
        load.start()

    barrier = pltpu.get_barrier_semaphore()
    for k in range(1, groups):
        pl.semaphore_signal(barrier, inc=1, device_id=(lax.rem(t + k, groups), s), device_id_type=MESH)

    @pl.when(has_up)
    def _():
        for k in range(groups):
            pl.semaphore_signal(barrier, inc=1, device_id=(lax.rem(t + k, groups), s - 1), device_id_type=MESH)

    @pl.when(has_down)
    def _():
        for k in range(groups):
            pl.semaphore_signal(barrier, inc=1, device_id=(lax.rem(t + k, groups), s + 1), device_id_type=MESH)

    near = 3 - jnp.where(has_up, 0, 1) - jnp.where(has_down, 0, 1)

    for load in loads:
        load.wait()
    for r in range(0, 16, 8):
        before = zero
        for b in range(blocks):
            turned = pltpu.roll(stage[0, r : r + 8, b * L : (b + 1) * L], H, 1)
            shifted[b, r : r + 8, :] = jnp.where(lane < H, before, turned)
            before = turned
        shifted[blocks, r : r + 8, :] = jnp.where(lane < H, before, 0.0)

    def around(ref, a, rows, count, per):
        values = []
        for n in range(-1, count + 1):
            at = jnp.clip(t * per + n, 0, per * groups - 1)
            cols = pl.ds(pl.multiple_of(at * L, L), L)
            value = ref[rows, cols] if a is None else ref[a, rows, cols]
            if n < 0:
                value = jnp.where(t == 0, 0.0, value)
            if n == count:
                value = jnp.where(t == last, 0.0, value)
            values.append(value)
        return values

    for a in range(3):
        for r in range(0, 16, 8):
            turned = [pltpu.roll(v, H, 1) for v in around(stage, 1 + a, slice(r, r + 8), width, width)]
            for i in range(wb):
                co[a, i, TOP + r : TOP + r + 8, :] = jnp.where(lane < H, turned[i], turned[i + 1])
    pl.semaphore_wait(barrier, groups * near - 1)

    def guess_copy(k, part, where):
        c = lax.rem(t - k + groups, groups)
        mine = (slice(0, 16), slice(8, 16), slice(0, 8))[part]
        there = (MAIN, UP, DOWN)[part]
        return remote(
            shifted.at[pl.ds(width * c, wb), mine, :], guess.at[k, :, there, :],
            g_send.at[part, k], g_recv.at[part, k], where or (c, s + (0, 1, -1)[part]),
        )

    send(has_down, remote(co.at[:, :, TOP + 8 : TOP + 16, :], co.at[:, :, UP, :], c_send.at[0], c_recv.at[0], (t, s + 1)))
    send(has_up, remote(co.at[:, :, TOP : TOP + 8, :], co.at[:, :, DOWN, :], c_send.at[1], c_recv.at[1], (t, s - 1)))
    def send_guesses(slots):
        for k in slots:
            send((t < last) & has_down, guess_copy(k, 1, None))
            send((t < last) & has_up, guess_copy(k, 2, None))
            if k > 0:
                send(t < last, guess_copy(k, 0, None))

    send_guesses(ROUNDS[0])
    if not SPLIT:
        send_guesses(ROUNDS[1])

    turned = [pltpu.roll(v, H // 2, 1) for v in around(flow_stage, None, slice(0, 8), cwidth, cwidth)]
    for i in range(cwidth + 1):
        value = jnp.where(lane < H // 2, turned[i], turned[i + 1])
        for a in range(3):
            if a > 0:
                value = restrict_block(co.at[a - 1], i, TOP, lane)
            wsrc[a, i, :, :] = value
            win[a, i, 16:24, :] = value
    w_down = remote(wsrc, win.at[:, :, 8:16, :], w_send.at[0], w_recv.at[0], (t, s + 1))
    w_up = remote(wsrc, win.at[:, :, 24:32, :], w_send.at[1], w_recv.at[1], (t, s - 1))
    send(has_down, w_down)
    send(has_up, w_up)

    def clear(fine, coarse, halo):
        for i in range(wb):
            for a in range(3):
                co[a, i, fine, :] = zero
            for k in range(groups):
                guess[k, i, fine, :] = zero
        for i in range(cwidth + 1):
            for a in range(3):
                win[a, i, coarse, :] = zero
            for j in range(groups):
                rd[j, i, halo, :] = zero

    @pl.when(~has_up)
    def _():
        clear(UP, slice(8, 16), slice(0, 8))

    @pl.when(~has_down)
    def _():
        clear(DOWN, slice(24, 32), slice(16, 24))

    for i in range(wb):
        guess[0, i, MAIN, :] = shifted[width * t + i, :, :]

    if SPLIT:
        drain()
        send_guesses(ROUNDS[1])

    @pl.when(has_up)
    def _():
        remote(co.at[:, :, TOP + 8 : TOP + 16, :], co.at[:, :, UP, :], c_send.at[0], c_recv.at[0], (t, s)).wait_recv()
        remote(wsrc, win.at[:, :, 8:16, :], w_send.at[0], w_recv.at[0], (t, s)).wait_recv()

    @pl.when(has_down)
    def _():
        remote(co.at[:, :, TOP : TOP + 8, :], co.at[:, :, DOWN, :], c_send.at[1], c_recv.at[1], (t, s)).wait_recv()
        remote(wsrc, win.at[:, :, 24:32, :], w_send.at[1], w_recv.at[1], (t, s)).wait_recv()

    def arrive(k):
        held = lax.rem(t + k, groups) < last

        @pl.when(held & has_up)
        def _():
            guess_copy(k, 1, (t, s)).wait_recv()

        @pl.when(held & has_down)
        def _():
            guess_copy(k, 2, (t, s)).wait_recv()

        if k > 0:
            @pl.when(held)
            def _():
                guess_copy(k, 0, (t, s)).wait_recv()

    step = functools.partial(fine_step, co=co, last_strip=~has_down, last_window=t == last)
    for pair in ROUNDS:
        for k in pair:
            arrive(k)
        g0, r0 = [guess.at[k] for k in pair], [relaxed.at[k] for k in pair]
        a0, b0 = [ua.at[n] for n in range(len(pair))], [ub.at[n] for n in range(len(pair))]
        for src, dst, first, tiles in (
            (g0, a0, -8, 4), (a0, b0, -8, 4), (b0, a0, -8, 4), (a0, r0, -4, 3),
            (r0, a0, -4, 3), (a0, b0, -4, 3), (b0, a0, -4, 3), (a0, b0, 0, 2),
        ):
            step(list(zip(src, dst)), first=TOP + first, tiles=tiles)
        for n, k in enumerate(pair):
            o = lax.rem(t + k, groups) + 1
            for i in range(cwidth + 1):
                tcoarse[o, i, 7:15, :] = restrict_block(relaxed.at[k], i, TOP - 2, lane)
                value = restrict_block(relaxed.at[k], i, TOP + 2, lane)
                tcoarse[o, i, 9:17, :] = jnp.where((row == 7) & ~has_down, 0.0, value)
        for n, k in enumerate(pair):
            o = lax.rem(t + k, groups) + 1
            turned = zero
            for i in range(cwidth + 1):
                u = tcoarse[o, i, 8:16, :]
                rn = pltpu.roll(tcoarse[o, i + 1, 8:16, :], L - 1, 1) if i < cwidth else zero
                right = jnp.where(lane == L - 1, rn, pltpu.roll(u, L - 1, 1))
                change, turned = fluxes(
                    u, right, tcoarse[o, i, 7:15, :], tcoarse[o, i, 9:17, :],
                    win[1, i, 16:24, :], win[1, i, 15:23, :], win[2, i, 16:24, :], turned, lane,
                )
                rd[o, i, 8:16, :] = restrict_block(ub.at[n], i, TOP, lane) - (u + change)
    for i in range(cwidth + 1):
        rd[0, i, 8:16, :] = tcoarse[1, i, 8:16, :]

    def d_copy(j, part, where):
        halo = last - 1 - j
        mine = (slice(16 - halo, 16), slice(8, 8 + halo))[part]
        there = (slice(8 - halo, 8), slice(16, 16 + halo))[part]
        both = slice(j, j + 2)
        return remote(rd.at[both, :, mine, :], rd.at[both, :, there, :], d_send.at[part, j], d_recv.at[part, j], where)

    for j in range(0, last - 1, 2):
        send(has_down, d_copy(j, 0, (t, s + 1)))
        send(has_up, d_copy(j, 1, (t, s - 1)))

    for g in range(groups):
        k = lax.rem(g - 1 - t + 2 * groups, groups) if g > 0 else lax.rem(groups - t, groups)
        ref = relaxed if g > 0 else guess
        for r in range(0, 16, 8):
            turned = [pltpu.roll(ref[k, i, TOP + r : TOP + r + 8, :], H, 1) for i in range(wb)]
            for i in range(width):
                outw[g, r : r + 8, i * L : (i + 1) * L] = jnp.where(lane < H, turned[i], turned[i + 1])

    def finish(g, error):
        for i in range(width):
            base = H // 2 + H * i
            at = base % L + lane // 2
            wide = gather(error[base // L], at % L, 1)
            if base % L + H > L:
                wide = jnp.where(at < L, wide, gather(error[base // L + 1], at % L, 1))
            for p in range(2):
                tall = gather(wide, row // 2 + 4 * p, 0)
                rows, cols = slice(8 * p, 8 * p + 8), slice(i * L, (i + 1) * L)
                outw[g, rows, cols] = outw[g, rows, cols] + tall

    def send_windows(start, stop):
        for g in range(start, stop):
            send(t != g, out_copy(g, t, (g, s)))

            @pl.when(t == g)
            def _():
                own_copy(g).start()

    def out_copy(g, c, where):
        cols = pl.ds(pl.multiple_of(c * (width * L), L), width * L)
        return remote(outw.at[g], out_hbm.at[0, :, cols], o_send.at[g], o_recv.at[c], where)

    def own_copy(g):
        cols = pl.ds(pl.multiple_of(t * (width * L), L), width * L)
        return pltpu.make_async_copy(outw.at[g], out_hbm.at[0, :, cols], own_sem)

    finish(0, [win[0, i, 16:24, :] for i in range(cwidth + 1)])
    send_windows(0, 1)

    keep = {}
    for k in range(3):
        for i in range(cwidth + 1):
            bad = jnp.broadcast_to(~has_down, (8, L)) if k == 2 else None
            if i == cwidth:
                beyond = (lane >= H // 2) & (t == last)
                bad = beyond if bad is None else bad | beyond
            keep[k, i] = bad
    for j in range(0, last - 1, 2):
        @pl.when(has_up)
        def _():
            d_copy(j, 0, (t, s)).wait_recv()

        @pl.when(has_down)
        def _():
            d_copy(j, 1, (t, s)).wait_recv()

    now, later = win.at[0], fa
    for g in range(1, groups):
        j = g - 1
        error = []
        for k in range(3):
            if g == last and k != 1:
                continue
            r = 8 + 8 * k
            turned = zero
            for i in range(cwidth + 1):
                u = now[i, r : r + 8, :]
                rn = pltpu.roll(now[i + 1, r : r + 8, :], L - 1, 1) if i < cwidth else zero
                right = jnp.where(lane == L - 1, rn, pltpu.roll(u, L - 1, 1))
                change, turned = fluxes(
                    u, right, now[i, r - 1 : r + 7, :], now[i, r + 1 : r + 9, :],
                    win[1, i, r : r + 8, :], win[1, i, r - 1 : r + 7, :], win[2, i, r : r + 8, :], turned, lane,
                )
                value = u + change + rd[j, i, 8 * k : 8 * k + 8, :]
                if keep[k, i] is not None:
                    value = jnp.where(keep[k, i], 0.0, value)
                if g < last:
                    later[i, r : r + 8, :] = value
                if k == 1:
                    error.append(value - tcoarse[g, i, 8:16, :])
        now, later = later, (fb if later is fa else fa)
        finish(g, error)
        if g in BATCHES:
            send_windows(max([1] + [b + 1 for b in BATCHES if b < g]), g + 1)

    for c in range(groups):
        @pl.when(t != c)
        def _():
            out_copy(0, c, (t, s)).wait_recv()

    drain()
    own_copy(0).wait()


def solution(mesh):
    groups, strips = mesh.shape["tm"], mesh.shape["space"]

    def shards(guesses, cond_x, cond_y, source, inflow):
        _, rows, columns = guesses.shape
        blocks = columns // L
        assert rows == 16 and groups == 8 and blocks == 4 * groups
        vmem = lambda *shape: pltpu.VMEM(shape, F32)
        dma = lambda *shape: pltpu.SemaphoreType.DMA(shape)
        return pl.pallas_call(
            functools.partial(kernel, groups, strips),
            out_shape=jax.ShapeDtypeStruct(guesses.shape, F32),
            in_specs=[pl.BlockSpec(memory_space=pl.ANY)] * 5,
            out_specs=pl.BlockSpec(memory_space=pl.ANY),
            scratch_shapes=[
                vmem(4, rows, columns), vmem(rows // 2, columns // 2), vmem(blocks + 1, rows, L),
                vmem(groups, 5, 48, L), vmem(groups, 5, 48, L), vmem(4, 5, 48, L), vmem(4, 5, 48, L),
                vmem(3, 5, 48, L), vmem(groups + 1, 3, 24, L), vmem(3, 3, 8, L), vmem(3, 3, 40, L),
                vmem(groups + 1, 3, 24, L), vmem(3, 40, L), vmem(3, 40, L), vmem(groups, rows, 4 * L),
                dma(5), dma(3, groups), dma(3, groups), dma(2), dma(2), dma(2), dma(2),
                dma(2, groups), dma(2, groups), dma(groups), dma(groups), pltpu.SemaphoreType.DMA,
            ],
            compiler_params=pltpu.CompilerParams(
                collective_id=0, has_side_effects=True, vmem_limit_bytes=60 * 2**20
            ),
        )(guesses, cond_x, cond_y, source, inflow)

    return jax.shard_map(
        shards,
        mesh=mesh,
        in_specs=(
            P("tm", "space", None),
            P("space", None),
            P("space", None),
            P("space", None),
            P("space", None),
        ),
        out_specs=P("tm", "space", None),
        check_vma=False,
    )
```

```python
import functools

import jax
import jax.numpy as jnp
from jax import lax
from jax.experimental import pallas as pl
from jax.experimental.pallas import tpu as pltpu
from jax.sharding import PartitionSpec as P

MESH = pl.DeviceIdType.MESH
F32 = jnp.float32
L = 128
H = L // 2
TOP = 16
UP, DOWN, MAIN = slice(TOP - 8, TOP), slice(TOP + 16, TOP + 24), slice(TOP, TOP + 16)
ORDER = (4, 3, 5, 2, 6, 1, 7, 0)
ROUNDS = ((0, 1, 2, 3, 4, 5, 6),)
BATCHES = (2, 4, 6, 7)


def remote(src, dst, send, recv, where):
    return pltpu.make_async_remote_copy(
        src_ref=src, dst_ref=dst, send_sem=send, recv_sem=recv, device_id=where, device_id_type=MESH
    )


def gather(value, index, axis):
    return jnp.take_along_axis(value, index, axis=axis, mode="promise_in_bounds")


def restrict_block(ref, block, row, lane):
    halves = []
    for q in range(2):
        if 2 * block + q >= ref.shape[0]:
            halves.append(jnp.zeros((8, L), F32))
            continue
        pair = ref[2 * block + q, pl.ds(row, 8, stride=2), :] + ref[
            2 * block + q, pl.ds(row + 1, 8, stride=2), :
        ]
        pair = pair + pltpu.roll(pair, L - 1, 1)
        halves.append(gather(pair, (2 * lane) % L, 1))
    return jnp.where(lane < H, halves[0], halves[1]) * 0.25


def fluxes(u, right, up, down, cx, cx_up, cy, carry, lane):
    flow = cy * (right - u)
    turned = pltpu.roll(flow, 1, 1)
    west = jnp.where(lane == 0, carry, turned)
    total = cx * (down - u) - cx_up * (u - up)
    return total + flow - west, turned


def fine_step(pairs, co, first, tiles, last_strip, last_window):
    cx, cy, source = (co.at[i] for i in range(3))
    blocks = co.shape[1]
    lane = lax.broadcasted_iota(jnp.int32, (8, L), 1)
    row = lax.broadcasted_iota(jnp.int32, (8, L), 0)
    zero = jnp.zeros((8, L), F32)
    rows = [first + 8 * k for k in range(tiles)]
    below = [None if r + 8 <= TOP + 16 else (row + r >= TOP + 16) & last_strip for r in rows]
    beyond = (lane >= H) & last_window
    state = {}
    for n, (src, _) in enumerate(pairs):
        for k, r in enumerate(rows):
            u = src[0, r : r + 8, :]
            state[n, k] = (u, pltpu.roll(u, L - 1, 1), zero)
    for b in range(blocks):
        for n, (src, dst) in enumerate(pairs):
            for k, r in enumerate(rows):
                u, ru, turned = state[n, k]
                nxt, rn = zero, zero
                if b + 1 < blocks:
                    nxt = src[b + 1, r : r + 8, :]
                    rn = pltpu.roll(nxt, L - 1, 1)
                right = jnp.where(lane == L - 1, rn, ru)
                change, turned = fluxes(
                    u, right, src[b, r - 1 : r + 7, :], src[b, r + 1 : r + 9, :],
                    cx[b, r : r + 8, :], cx[b, r - 1 : r + 7, :], cy[b, r : r + 8, :], turned, lane,
                )
                out = u + change + source[b, r : r + 8, :]
                drop = below[k]
                if b + 1 == blocks:
                    drop = beyond if drop is None else drop | beyond
                if drop is not None:
                    out = jnp.where(drop, 0.0, out)
                dst[b, r : r + 8, :] = out
                state[n, k] = (nxt, rn, turned)


def kernel(
    groups, strips, guess_in, cx_in, cy_in, source_in, inflow_in, out_hbm,
    stage, flow_stage, shifted, guess, relaxed, ua, ub, co, tcoarse, wsrc, win, rd, fa, fb, outw,
    in_sems, g_send, g_recv, c_send, c_recv, w_send, w_recv, d_send, d_recv, o_send, o_recv, own_sem,
):
    t = lax.axis_index("tm")
    s = lax.axis_index("space")
    has_up, has_down = s > 0, s < strips - 1
    last = groups - 1
    lane = lax.broadcasted_iota(jnp.int32, (8, L), 1)
    row = lax.broadcasted_iota(jnp.int32, (8, L), 0)
    zero = jnp.zeros((8, L), F32)
    blocks = shifted.shape[0] - 1
    width = blocks // groups
    cwidth = width // 2
    wb = width + 1
    sends = []

    def send(cond, copy):
        sends.append((cond, copy))

        @pl.when(cond)
        def _():
            copy.start()

    def drain():
        for cond, copy in sends:
            @pl.when(cond)
            def _(copy=copy):
                copy.wait_send()
        sends.clear()

    loads = [
        pltpu.make_async_copy(ref, stage.at[i], in_sems.at[i])
        for i, ref in enumerate((guess_in.at[0], cx_in, cy_in, source_in))
    ]
    loads.append(pltpu.make_async_copy(inflow_in, flow_stage, in_sems.at[4]))
    for load in loads:
        load.start()

    barrier = pltpu.get_barrier_semaphore()
    for k in range(1, groups):
        pl.semaphore_signal(barrier, inc=1, device_id=(lax.rem(t + k, groups), s), device_id_type=MESH)

    @pl.when(has_up)
    def _():
        for k in range(groups):
            pl.semaphore_signal(barrier, inc=1, device_id=(lax.rem(t + k, groups), s - 1), device_id_type=MESH)

    @pl.when(has_down)
    def _():
        for k in range(groups):
            pl.semaphore_signal(barrier, inc=1, device_id=(lax.rem(t + k, groups), s + 1), device_id_type=MESH)

    near = 3 - jnp.where(has_up, 0, 1) - jnp.where(has_down, 0, 1)

    loads[0].wait()
    for r in range(0, 16, 8):
        before = zero
        for b in range(blocks):
            turned = pltpu.roll(stage[0, r : r + 8, b * L : (b + 1) * L], H, 1)
            shifted[b, r : r + 8, :] = jnp.where(lane < H, before, turned)
            before = turned
        shifted[blocks, r : r + 8, :] = jnp.where(lane < H, before, 0.0)

    def around(ref, a, rows, count, per):
        values = []
        for n in range(-1, count + 1):
            at = jnp.clip(t * per + n, 0, per * groups - 1)
            cols = pl.ds(pl.multiple_of(at * L, L), L)
            value = ref[rows, cols] if a is None else ref[a, rows, cols]
            if n < 0:
                value = jnp.where(t == 0, 0.0, value)
            if n == count:
                value = jnp.where(t == last, 0.0, value)
            values.append(value)
        return values

    pl.semaphore_wait(barrier, groups * near - 1)

    def guess_copy(g, k, part, where):
        c = lax.rem(t + k, groups)
        mine = (slice(0, 16), slice(8, 16), slice(0, 8))[part]
        there = (MAIN, UP, DOWN)[part]
        return remote(
            shifted.at[pl.ds(width * c, wb), mine, :], guess.at[g, :, there, :],
            g_send.at[part, k], g_recv.at[part, g], where or (c, s + (0, 1, -1)[part]),
        )

    for k in ORDER:
        send((t < last) & has_down, guess_copy(t, k, 1, None))
        send((t < last) & has_up, guess_copy(t, k, 2, None))
        if k > 0:
            send(t < last, guess_copy(t, k, 0, None))

    for load in loads[1:]:
        load.wait()
    for a in range(3):
        for r in range(0, 16, 8):
            turned = [pltpu.roll(v, H, 1) for v in around(stage, 1 + a, slice(r, r + 8), width, width)]
            for i in range(wb):
                co[a, i, TOP + r : TOP + r + 8, :] = jnp.where(lane < H, turned[i], turned[i + 1])
    send(has_down, remote(co.at[:, :, TOP + 8 : TOP + 16, :], co.at[:, :, UP, :], c_send.at[0], c_recv.at[0], (t, s + 1)))
    send(has_up, remote(co.at[:, :, TOP : TOP + 8, :], co.at[:, :, DOWN, :], c_send.at[1], c_recv.at[1], (t, s - 1)))

    turned = [pltpu.roll(v, H // 2, 1) for v in around(flow_stage, None, slice(0, 8), cwidth, cwidth)]
    for i in range(cwidth + 1):
        value = jnp.where(lane < H // 2, turned[i], turned[i + 1])
        for a in range(3):
            if a > 0:
                value = restrict_block(co.at[a - 1], i, TOP, lane)
            wsrc[a, i, :, :] = value
            win[a, i, 16:24, :] = value
    w_down = remote(wsrc, win.at[:, :, 8:16, :], w_send.at[0], w_recv.at[0], (t, s + 1))
    w_up = remote(wsrc, win.at[:, :, 24:32, :], w_send.at[1], w_recv.at[1], (t, s - 1))
    send(has_down, w_down)
    send(has_up, w_up)

    def clear(fine, coarse, halo):
        for i in range(wb):
            for a in range(3):
                co[a, i, fine, :] = zero
            for g in range(last):
                guess[g, i, fine, :] = zero
        for i in range(cwidth + 1):
            for a in range(3):
                win[a, i, coarse, :] = zero
            for j in range(groups):
                rd[j, i, halo, :] = zero

    @pl.when(~has_up)
    def _():
        clear(UP, slice(8, 16), slice(0, 8))

    @pl.when(~has_down)
    def _():
        clear(DOWN, slice(24, 32), slice(16, 24))

    @pl.when(t < last)
    def _():
        for i in range(wb):
            guess[t, i, MAIN, :] = shifted[width * t + i, :, :]

    @pl.when(has_up)
    def _():
        remote(co.at[:, :, TOP + 8 : TOP + 16, :], co.at[:, :, UP, :], c_send.at[0], c_recv.at[0], (t, s)).wait_recv()
        remote(wsrc, win.at[:, :, 8:16, :], w_send.at[0], w_recv.at[0], (t, s)).wait_recv()

    @pl.when(has_down)
    def _():
        remote(co.at[:, :, TOP : TOP + 8, :], co.at[:, :, DOWN, :], c_send.at[1], c_recv.at[1], (t, s)).wait_recv()
        remote(wsrc, win.at[:, :, 24:32, :], w_send.at[1], w_recv.at[1], (t, s)).wait_recv()

    def arrive(g):
        @pl.when(has_up)
        def _():
            guess_copy(g, 0, 1, (t, s)).wait_recv()

        @pl.when(has_down)
        def _():
            guess_copy(g, 0, 2, (t, s)).wait_recv()

        @pl.when(t != g)
        def _():
            guess_copy(g, 0, 0, (t, s)).wait_recv()

    step = functools.partial(fine_step, co=co, last_strip=~has_down, last_window=t == last)
    for part in ROUNDS:
        for k in part:
            arrive(k)
        g0, r0 = [guess.at[k] for k in part], [relaxed.at[k] for k in part]
        a0, b0 = [ua.at[n] for n in range(len(part))], [ub.at[n] for n in range(len(part))]
        first_pass_done = False
        for src, dst, first, tiles in (
            (g0, a0, -8, 4), (a0, b0, -8, 4), (b0, a0, -8, 4), (a0, r0, -4, 3),
            (r0, a0, -4, 3), (a0, b0, -4, 3), (b0, a0, -4, 3), (a0, b0, 0, 2),
        ):
            both = list(zip(src, dst))
            if src is r0 or first_pass_done:
                first_pass_done = True
                both = [pair for k, pair in zip(part, both) if k < last - 1]
            step(both, first=TOP + first, tiles=tiles)
        for i in range(cwidth + 1):
            for n, k in enumerate(part):
                o = k + 1
                tcoarse[o, i, 7:15, :] = restrict_block(relaxed.at[k], i, TOP - 2, lane)
                value = restrict_block(relaxed.at[k], i, TOP + 2, lane)
                tcoarse[o, i, 9:17, :] = jnp.where((row == 7) & ~has_down, 0.0, value)
        turned = {k: zero for k in part}
        for i in range(cwidth + 1):
            for n, k in enumerate(part):
                o = k + 1
                if o == last:
                    continue
                u = tcoarse[o, i, 8:16, :]
                rn = pltpu.roll(tcoarse[o, i + 1, 8:16, :], L - 1, 1) if i < cwidth else zero
                right = jnp.where(lane == L - 1, rn, pltpu.roll(u, L - 1, 1))
                change, turned[k] = fluxes(
                    u, right, tcoarse[o, i, 7:15, :], tcoarse[o, i, 9:17, :],
                    win[1, i, 16:24, :], win[1, i, 15:23, :], win[2, i, 16:24, :], turned[k], lane,
                )
                rd[o, i, 8:16, :] = restrict_block(ub.at[n], i, TOP, lane) - (u + change)
    for i in range(cwidth + 1):
        rd[0, i, 8:16, :] = tcoarse[1, i, 8:16, :]

    def d_copy(j, part, where):
        halo = last - 1 - j
        mine = (slice(16 - halo, 16), slice(8, 8 + halo))[part]
        there = (slice(8 - halo, 8), slice(16, 16 + halo))[part]
        both = slice(j, j + 2)
        return remote(rd.at[both, :, mine, :], rd.at[both, :, there, :], d_send.at[part, j], d_recv.at[part, j], where)

    for j in range(0, last - 1, 2):
        send(has_down, d_copy(j, 0, (t, s + 1)))
        send(has_up, d_copy(j, 1, (t, s - 1)))

    for g in range(groups):
        k = max(g - 1, 0)
        ref = relaxed if g > 0 else guess
        for r in range(0, 16, 8):
            turned = [pltpu.roll(ref[k, i, TOP + r : TOP + r + 8, :], H, 1) for i in range(wb)]
            for i in range(width):
                outw[g, r : r + 8, i * L : (i + 1) * L] = jnp.where(lane < H, turned[i], turned[i + 1])

    def finish(g, error):
        for i in range(width):
            base = H // 2 + H * i
            at = base % L + lane // 2
            wide = gather(error[base // L], at % L, 1)
            if base % L + H > L:
                wide = jnp.where(at < L, wide, gather(error[base // L + 1], at % L, 1))
            for p in range(2):
                tall = gather(wide, row // 2 + 4 * p, 0)
                rows, cols = slice(8 * p, 8 * p + 8), slice(i * L, (i + 1) * L)
                outw[g, rows, cols] = outw[g, rows, cols] + tall

    def send_windows(start, stop):
        for g in range(start, stop):
            send(t != g, out_copy(g, t, (g, s)))

            @pl.when(t == g)
            def _():
                own_copy(g).start()

    def out_copy(g, c, where):
        cols = pl.ds(pl.multiple_of(c * (width * L), L), width * L)
        return remote(outw.at[g], out_hbm.at[0, :, cols], o_send.at[g], o_recv.at[c], where)

    def own_copy(g):
        cols = pl.ds(pl.multiple_of(t * (width * L), L), width * L)
        return pltpu.make_async_copy(outw.at[g], out_hbm.at[0, :, cols], own_sem)

    finish(0, [win[0, i, 16:24, :] for i in range(cwidth + 1)])
    send_windows(0, 1)

    keep = {}
    for k in range(3):
        for i in range(cwidth + 1):
            bad = jnp.broadcast_to(~has_down, (8, L)) if k == 2 else None
            if i == cwidth:
                beyond = (lane >= H // 2) & (t == last)
                bad = beyond if bad is None else bad | beyond
            keep[k, i] = bad
    for j in range(0, last - 1, 2):
        @pl.when(has_up)
        def _():
            d_copy(j, 0, (t, s)).wait_recv()

        @pl.when(has_down)
        def _():
            d_copy(j, 1, (t, s)).wait_recv()

    now, later = win.at[0], fa
    for g in range(1, groups):
        j = g - 1
        error = []
        for k in range(3):
            if g == last and k != 1:
                continue
            r = 8 + 8 * k
            turned = zero
            for i in range(cwidth + 1):
                u = now[i, r : r + 8, :]
                rn = pltpu.roll(now[i + 1, r : r + 8, :], L - 1, 1) if i < cwidth else zero
                right = jnp.where(lane == L - 1, rn, pltpu.roll(u, L - 1, 1))
                change, turned = fluxes(
                    u, right, now[i, r - 1 : r + 7, :], now[i, r + 1 : r + 9, :],
                    win[1, i, r : r + 8, :], win[1, i, r - 1 : r + 7, :], win[2, i, r : r + 8, :], turned, lane,
                )
                value = u + change + rd[j, i, 8 * k : 8 * k + 8, :]
                if keep[k, i] is not None:
                    value = jnp.where(keep[k, i], 0.0, value)
                if g < last:
                    later[i, r : r + 8, :] = value
                if k == 1:
                    error.append(value - tcoarse[g, i, 8:16, :])
        now, later = later, (fb if later is fa else fa)
        finish(g, error)
        if g in BATCHES:
            send_windows(max([1] + [b + 1 for b in BATCHES if b < g]), g + 1)

    for c in range(groups):
        @pl.when(t != c)
        def _():
            out_copy(0, c, (t, s)).wait_recv()

    drain()
    own_copy(0).wait()


def solution(mesh):
    groups, strips = mesh.shape["tm"], mesh.shape["space"]

    def shards(guesses, cond_x, cond_y, source, inflow):
        _, rows, columns = guesses.shape
        blocks = columns // L
        assert rows == 16 and groups == 8 and blocks == 4 * groups
        vmem = lambda *shape: pltpu.VMEM(shape, F32)
        dma = lambda *shape: pltpu.SemaphoreType.DMA(shape)
        return pl.pallas_call(
            functools.partial(kernel, groups, strips),
            out_shape=jax.ShapeDtypeStruct(guesses.shape, F32),
            in_specs=[pl.BlockSpec(memory_space=pl.ANY)] * 5,
            out_specs=pl.BlockSpec(memory_space=pl.ANY),
            scratch_shapes=[
                vmem(4, rows, columns), vmem(rows // 2, columns // 2), vmem(blocks + 1, rows, L),
                vmem(groups - 1, 5, 48, L), vmem(groups - 1, 5, 48, L), vmem(groups - 1, 5, 48, L), vmem(groups - 1, 5, 48, L),
                vmem(3, 5, 48, L), vmem(groups, 3, 24, L), vmem(3, 3, 8, L), vmem(3, 3, 40, L),
                vmem(groups, 3, 24, L), vmem(3, 40, L), vmem(3, 40, L), vmem(groups, rows, 4 * L),
                dma(5), dma(3, groups), dma(3, groups), dma(2), dma(2), dma(2), dma(2),
                dma(2, groups), dma(2, groups), dma(groups), dma(groups), pltpu.SemaphoreType.DMA,
            ],
            compiler_params=pltpu.CompilerParams(
                collective_id=0, has_side_effects=True, vmem_limit_bytes=60 * 2**20
            ),
        )(guesses, cond_x, cond_y, source, inflow)

    return jax.shard_map(
        shards,
        mesh=mesh,
        in_specs=(
            P("tm", "space", None),
            P("space", None),
            P("space", None),
            P("space", None),
            P("space", None),
        ),
        out_specs=P("tm", "space", None),
        check_vma=False,
    )
```

```python
import functools

import jax
import jax.numpy as jnp
from jax import lax
from jax.experimental import pallas as pl
from jax.experimental.pallas import tpu as pltpu
from jax.sharding import PartitionSpec as P

MESH = pl.DeviceIdType.MESH
F32 = jnp.float32
L = 128
H = L // 2
TOP = 16
UP, DOWN, MAIN = slice(TOP - 8, TOP), slice(TOP + 16, TOP + 24), slice(TOP, TOP + 16)
ORDER = (4, 3, 5, 2, 6, 1, 7, 0)
ROUNDS = ((0, 1, 2, 3, 4, 5, 6),)
BATCHES = (2, 4, 6, 7)


def remote(src, dst, send, recv, where):
    return pltpu.make_async_remote_copy(
        src_ref=src, dst_ref=dst, send_sem=send, recv_sem=recv, device_id=where, device_id_type=MESH
    )


def gather(value, index, axis):
    return jnp.take_along_axis(value, index, axis=axis, mode="promise_in_bounds")


def restrict_block(ref, block, row, lane):
    halves = []
    for q in range(2):
        if 2 * block + q >= ref.shape[0]:
            halves.append(jnp.zeros((8, L), F32))
            continue
        pair = ref[2 * block + q, pl.ds(row, 8, stride=2), :] + ref[
            2 * block + q, pl.ds(row + 1, 8, stride=2), :
        ]
        pair = pair + pltpu.roll(pair, L - 1, 1)
        halves.append(gather(pair, (2 * lane) % L, 1))
    return jnp.where(lane < H, halves[0], halves[1]) * 0.25


def fluxes(u, right, up, down, cx, cx_up, cy, carry, lane):
    flow = cy * (right - u)
    turned = pltpu.roll(flow, 1, 1)
    west = jnp.where(lane == 0, carry, turned)
    total = cx * (down - u) - cx_up * (u - up)
    return total + flow - west, turned


def fine_step(pairs, co, first, tiles, last_strip, last_window):
    cx, cy, source = (co.at[i] for i in range(3))
    blocks = co.shape[1]
    lane = lax.broadcasted_iota(jnp.int32, (8, L), 1)
    row = lax.broadcasted_iota(jnp.int32, (8, L), 0)
    zero = jnp.zeros((8, L), F32)
    rows = [first + 8 * k for k in range(tiles)]
    below = [None if r + 8 <= TOP + 16 else (row + r >= TOP + 16) & last_strip for r in rows]
    beyond = (lane >= H) & last_window
    state = {}
    for n, (src, _) in enumerate(pairs):
        for k, r in enumerate(rows):
            u = src[0, r : r + 8, :]
            state[n, k] = (u, pltpu.roll(u, L - 1, 1), zero)
    for b in range(blocks):
        for n, (src, dst) in enumerate(pairs):
            for k, r in enumerate(rows):
                u, ru, turned = state[n, k]
                nxt, rn = zero, zero
                if b + 1 < blocks:
                    nxt = src[b + 1, r : r + 8, :]
                    rn = pltpu.roll(nxt, L - 1, 1)
                right = jnp.where(lane == L - 1, rn, ru)
                change, turned = fluxes(
                    u, right, src[b, r - 1 : r + 7, :], src[b, r + 1 : r + 9, :],
                    cx[b, r : r + 8, :], cx[b, r - 1 : r + 7, :], cy[b, r : r + 8, :], turned, lane,
                )
                out = u + change + source[b, r : r + 8, :]
                drop = below[k]
                if b + 1 == blocks:
                    drop = beyond if drop is None else drop | beyond
                if drop is not None:
                    out = jnp.where(drop, 0.0, out)
                dst[b, r : r + 8, :] = out
                state[n, k] = (nxt, rn, turned)


def kernel(
    groups, strips, guess_in, cx_in, cy_in, source_in, inflow_in, out_hbm,
    stage, flow_stage, shifted, guess, relaxed, ua, ub, co, tcoarse, wsrc, win, rd, fa, fb, outw,
    in_sems, g_send, g_recv, c_send, c_recv, w_send, w_recv, d_send, d_recv, o_send, o_recv, own_sem,
):
    t = lax.axis_index("tm")
    s = lax.axis_index("space")
    has_up, has_down = s > 0, s < strips - 1
    last = groups - 1
    lane = lax.broadcasted_iota(jnp.int32, (8, L), 1)
    row = lax.broadcasted_iota(jnp.int32, (8, L), 0)
    zero = jnp.zeros((8, L), F32)
    blocks = shifted.shape[0] - 1
    width = blocks // groups
    cwidth = width // 2
    wb = width + 1
    sends = []

    def send(cond, copy):
        sends.append((cond, copy))

        @pl.when(cond)
        def _():
            copy.start()

    def drain():
        for cond, copy in sends:
            @pl.when(cond)
            def _(copy=copy):
                copy.wait_send()
        sends.clear()

    loads = [
        pltpu.make_async_copy(ref, stage.at[i], in_sems.at[i])
        for i, ref in enumerate((guess_in.at[0], cx_in, cy_in, source_in))
    ]
    loads.append(pltpu.make_async_copy(inflow_in, flow_stage, in_sems.at[4]))
    for load in loads:
        load.start()

    barrier = pltpu.get_barrier_semaphore()
    for k in range(1, groups):
        pl.semaphore_signal(barrier, inc=1, device_id=(lax.rem(t + k, groups), s), device_id_type=MESH)

    @pl.when(has_up)
    def _():
        for k in range(groups):
            pl.semaphore_signal(barrier, inc=1, device_id=(lax.rem(t + k, groups), s - 1), device_id_type=MESH)

    @pl.when(has_down)
    def _():
        for k in range(groups):
            pl.semaphore_signal(barrier, inc=1, device_id=(lax.rem(t + k, groups), s + 1), device_id_type=MESH)

    near = 3 - jnp.where(has_up, 0, 1) - jnp.where(has_down, 0, 1)

    loads[0].wait()
    for r in range(0, 16, 8):
        before = zero
        for b in range(blocks):
            turned = pltpu.roll(stage[0, r : r + 8, b * L : (b + 1) * L], H, 1)
            shifted[b, r : r + 8, :] = jnp.where(lane < H, before, turned)
            before = turned
        shifted[blocks, r : r + 8, :] = jnp.where(lane < H, before, 0.0)

    def around(ref, a, rows, count, per):
        values = []
        for n in range(-1, count + 1):
            at = jnp.clip(t * per + n, 0, per * groups - 1)
            cols = pl.ds(pl.multiple_of(at * L, L), L)
            value = ref[rows, cols] if a is None else ref[a, rows, cols]
            if n < 0:
                value = jnp.where(t == 0, 0.0, value)
            if n == count:
                value = jnp.where(t == last, 0.0, value)
            values.append(value)
        return values

    pl.semaphore_wait(barrier, groups * near - 1)

    def guess_copy(g, k, part, where):
        c = lax.rem(t + k, groups)
        mine = (slice(0, 16), slice(8, 16), slice(0, 8))[part]
        there = (MAIN, UP, DOWN)[part]
        return remote(
            shifted.at[pl.ds(width * c, wb), mine, :], guess.at[g, :, there, :],
            g_send.at[part, k], g_recv.at[part, g], where or (c, s + (0, 1, -1)[part]),
        )

    for k in ORDER:
        send((t < last) & has_down, guess_copy(t, k, 1, None))
        send((t < last) & has_up, guess_copy(t, k, 2, None))
        if k > 0:
            send(t < last, guess_copy(t, k, 0, None))

    for load in loads[1:]:
        load.wait()
    for a in range(3):
        for r in range(0, 16, 8):
            turned = [pltpu.roll(v, H, 1) for v in around(stage, 1 + a, slice(r, r + 8), width, width)]
            for i in range(wb):
                co[a, i, TOP + r : TOP + r + 8, :] = jnp.where(lane < H, turned[i], turned[i + 1])
    send(has_down, remote(co.at[:, :, TOP + 8 : TOP + 16, :], co.at[:, :, UP, :], c_send.at[0], c_recv.at[0], (t, s + 1)))
    send(has_up, remote(co.at[:, :, TOP : TOP + 8, :], co.at[:, :, DOWN, :], c_send.at[1], c_recv.at[1], (t, s - 1)))

    turned = [pltpu.roll(v, H // 2, 1) for v in around(flow_stage, None, slice(0, 8), cwidth, cwidth)]
    for i in range(cwidth + 1):
        value = jnp.where(lane < H // 2, turned[i], turned[i + 1])
        for a in range(3):
            if a > 0:
                value = restrict_block(co.at[a - 1], i, TOP, lane)
            wsrc[a, i, :, :] = value
            win[a, i, 16:24, :] = value
    w_down = remote(wsrc, win.at[:, :, 8:16, :], w_send.at[0], w_recv.at[0], (t, s + 1))
    w_up = remote(wsrc, win.at[:, :, 24:32, :], w_send.at[1], w_recv.at[1], (t, s - 1))
    send(has_down, w_down)
    send(has_up, w_up)

    def clear(fine, coarse, halo):
        for i in range(wb):
            for a in range(3):
                co[a, i, fine, :] = zero
            for g in range(last):
                guess[g, i, fine, :] = zero
        for i in range(cwidth + 1):
            for a in range(3):
                win[a, i, coarse, :] = zero
            for j in range(groups):
                rd[j, i, halo, :] = zero

    @pl.when(~has_up)
    def _():
        clear(UP, slice(8, 16), slice(0, 8))

    @pl.when(~has_down)
    def _():
        clear(DOWN, slice(24, 32), slice(16, 24))

    @pl.when(t < last)
    def _():
        for i in range(wb):
            guess[t, i, MAIN, :] = shifted[width * t + i, :, :]

    @pl.when(has_up)
    def _():
        remote(co.at[:, :, TOP + 8 : TOP + 16, :], co.at[:, :, UP, :], c_send.at[0], c_recv.at[0], (t, s)).wait_recv()
        remote(wsrc, win.at[:, :, 8:16, :], w_send.at[0], w_recv.at[0], (t, s)).wait_recv()

    @pl.when(has_down)
    def _():
        remote(co.at[:, :, TOP : TOP + 8, :], co.at[:, :, DOWN, :], c_send.at[1], c_recv.at[1], (t, s)).wait_recv()
        remote(wsrc, win.at[:, :, 24:32, :], w_send.at[1], w_recv.at[1], (t, s)).wait_recv()

    def arrive(g):
        @pl.when(has_up)
        def _():
            guess_copy(g, 0, 1, (t, s)).wait_recv()

        @pl.when(has_down)
        def _():
            guess_copy(g, 0, 2, (t, s)).wait_recv()

        @pl.when(t != g)
        def _():
            guess_copy(g, 0, 0, (t, s)).wait_recv()

    step = functools.partial(fine_step, co=co, last_strip=~has_down, last_window=t == last)
    for part in ROUNDS:
        for k in part:
            arrive(k)
        g0, r0 = [guess.at[k] for k in part], [relaxed.at[k] for k in part]
        a0, b0 = [ua.at[n] for n in range(len(part))], [ub.at[n] for n in range(len(part))]
        first_pass_done = False
        for src, dst, first, tiles in (
            (g0, a0, -8, 4), (a0, b0, -8, 4), (b0, a0, -8, 4), (a0, r0, -4, 3),
            (r0, a0, -4, 3), (a0, b0, -4, 3), (b0, a0, -4, 3), (a0, b0, 0, 2),
        ):
            both = list(zip(src, dst))
            if src is r0 or first_pass_done:
                first_pass_done = True
                both = [pair for k, pair in zip(part, both) if k < last - 1]
            step(both, first=TOP + first, tiles=tiles)
        for i in range(cwidth + 1):
            for n, k in enumerate(part):
                o = k + 1
                tcoarse[o, i, 7:15, :] = restrict_block(relaxed.at[k], i, TOP - 2, lane)
                value = restrict_block(relaxed.at[k], i, TOP + 2, lane)
                tcoarse[o, i, 9:17, :] = jnp.where((row == 7) & ~has_down, 0.0, value)
        turned = {k: zero for k in part}
        for i in range(cwidth + 1):
            for n, k in enumerate(part):
                o = k + 1
                if o == last:
                    continue
                u = tcoarse[o, i, 8:16, :]
                rn = pltpu.roll(tcoarse[o, i + 1, 8:16, :], L - 1, 1) if i < cwidth else zero
                right = jnp.where(lane == L - 1, rn, pltpu.roll(u, L - 1, 1))
                change, turned[k] = fluxes(
                    u, right, tcoarse[o, i, 7:15, :], tcoarse[o, i, 9:17, :],
                    win[1, i, 16:24, :], win[1, i, 15:23, :], win[2, i, 16:24, :], turned[k], lane,
                )
                rd[o, i, 8:16, :] = restrict_block(ub.at[n], i, TOP, lane) - (u + change)
    for i in range(cwidth + 1):
        rd[0, i, 8:16, :] = tcoarse[1, i, 8:16, :]

    def d_copy(j, part, where):
        halo = last - 1 - j
        mine = (slice(16 - halo, 16), slice(8, 8 + halo))[part]
        there = (slice(8 - halo, 8), slice(16, 16 + halo))[part]
        both = slice(j, j + 2)
        return remote(rd.at[both, :, mine, :], rd.at[both, :, there, :], d_send.at[part, j], d_recv.at[part, j], where)

    for j in range(0, last - 1, 2):
        send(has_down, d_copy(j, 0, (t, s + 1)))
        send(has_up, d_copy(j, 1, (t, s - 1)))

    for g in range(groups):
        k = max(g - 1, 0)
        ref = relaxed if g > 0 else guess
        for r in range(0, 16, 8):
            turned = [pltpu.roll(ref[k, i, TOP + r : TOP + r + 8, :], H, 1) for i in range(wb)]
            for i in range(width):
                outw[g, r : r + 8, i * L : (i + 1) * L] = jnp.where(lane < H, turned[i], turned[i + 1])

    def finish(g, error):
        for i in range(width):
            base = H // 2 + H * i
            at = base % L + lane // 2
            wide = gather(error[base // L], at % L, 1)
            if base % L + H > L:
                wide = jnp.where(at < L, wide, gather(error[base // L + 1], at % L, 1))
            for p in range(2):
                tall = gather(wide, row // 2 + 4 * p, 0)
                rows, cols = slice(8 * p, 8 * p + 8), slice(i * L, (i + 1) * L)
                outw[g, rows, cols] = outw[g, rows, cols] + tall

    def send_windows(start, stop):
        for g in range(start, stop):
            send(t != g, out_copy(g, t, (g, s)))

            @pl.when(t == g)
            def _():
                own_copy(g).start()

    def out_copy(g, c, where):
        cols = pl.ds(pl.multiple_of(c * (width * L), L), width * L)
        return remote(outw.at[g], out_hbm.at[0, :, cols], o_send.at[g], o_recv.at[c], where)

    def own_copy(g):
        cols = pl.ds(pl.multiple_of(t * (width * L), L), width * L)
        return pltpu.make_async_copy(outw.at[g], out_hbm.at[0, :, cols], own_sem)

    finish(0, [win[0, i, 16:24, :] for i in range(cwidth + 1)])
    send_windows(0, 1)

    keep = {}
    for k in range(3):
        for i in range(cwidth + 1):
            bad = jnp.broadcast_to(~has_down, (8, L)) if k == 2 else None
            if i == cwidth:
                beyond = (lane >= H // 2) & (t == last)
                bad = beyond if bad is None else bad | beyond
            keep[k, i] = bad
    for j in range(0, last - 1, 2):
        @pl.when(has_up)
        def _():
            d_copy(j, 0, (t, s)).wait_recv()

        @pl.when(has_down)
        def _():
            d_copy(j, 1, (t, s)).wait_recv()

    now, later = win.at[0], fa
    for g in range(1, groups):
        j = g - 1
        error = []
        for k in range(3):
            if g == last and k != 1:
                continue
            r = 8 + 8 * k
            turned = zero
            for i in range(cwidth + 1):
                u = now[i, r : r + 8, :]
                rn = pltpu.roll(now[i + 1, r : r + 8, :], L - 1, 1) if i < cwidth else zero
                right = jnp.where(lane == L - 1, rn, pltpu.roll(u, L - 1, 1))
                change, turned = fluxes(
                    u, right, now[i, r - 1 : r + 7, :], now[i, r + 1 : r + 9, :],
                    win[1, i, r : r + 8, :], win[1, i, r - 1 : r + 7, :], win[2, i, r : r + 8, :], turned, lane,
                )
                value = u + change + rd[j, i, 8 * k : 8 * k + 8, :]
                if keep[k, i] is not None:
                    value = jnp.where(keep[k, i], 0.0, value)
                if g < last:
                    later[i, r : r + 8, :] = value
                if k == 1:
                    error.append(value - tcoarse[g, i, 8:16, :])
        now, later = later, (fb if later is fa else fa)
        finish(g, error)
        if g in BATCHES:
            send_windows(max([1] + [b + 1 for b in BATCHES if b < g]), g + 1)

    for c in range(groups):
        @pl.when(t != c)
        def _():
            out_copy(0, c, (t, s)).wait_recv()

    drain()
    own_copy(0).wait()


def solution(mesh):
    groups, strips = mesh.shape["tm"], mesh.shape["space"]

    def shards(guesses, cond_x, cond_y, source, inflow):
        _, rows, columns = guesses.shape
        blocks = columns // L
        assert rows == 16 and groups == 8 and blocks == 4 * groups
        vmem = lambda *shape: pltpu.VMEM(shape, F32)
        dma = lambda *shape: pltpu.SemaphoreType.DMA(shape)
        return pl.pallas_call(
            functools.partial(kernel, groups, strips),
            out_shape=jax.ShapeDtypeStruct(guesses.shape, F32),
            in_specs=[pl.BlockSpec(memory_space=pl.ANY)] * 5,
            out_specs=pl.BlockSpec(memory_space=pl.ANY),
            scratch_shapes=[
                vmem(4, rows, columns), vmem(rows // 2, columns // 2), vmem(blocks + 1, rows, L),
                vmem(groups - 1, 5, 48, L), vmem(groups - 1, 5, 48, L), vmem(groups - 1, 5, 48, L), vmem(groups - 1, 5, 48, L),
                vmem(3, 5, 48, L), vmem(groups, 3, 24, L), vmem(3, 3, 8, L), vmem(3, 3, 40, L),
                vmem(groups, 3, 24, L), vmem(3, 40, L), vmem(3, 40, L), vmem(groups, rows, 4 * L),
                dma(5), dma(3, groups), dma(3, groups), dma(2), dma(2), dma(2), dma(2),
                dma(2, groups), dma(2, groups), dma(groups), dma(groups), pltpu.SemaphoreType.DMA,
            ],
            compiler_params=pltpu.CompilerParams(
                collective_id=0, has_side_effects=True, vmem_limit_bytes=40 * 2**20
            ),
        )(*(pltpu.with_memory_space_constraint(x, pltpu.MemorySpace.HBM) for x in (guesses, cond_x, cond_y, source, inflow)))

    return jax.shard_map(
        shards,
        mesh=mesh,
        in_specs=(
            P("tm", "space", None),
            P("space", None),
            P("space", None),
            P("space", None),
            P("space", None),
        ),
        out_specs=P("tm", "space", None),
        check_vma=False,
    )
```

```python
import functools

import jax
import jax.numpy as jnp
from jax import lax
from jax.experimental import pallas as pl
from jax.experimental.pallas import tpu as pltpu
from jax.sharding import PartitionSpec as P

MESH = pl.DeviceIdType.MESH
F32 = jnp.float32
L = 128
H = L // 2
TOP = 16
UP, DOWN, MAIN = slice(TOP - 8, TOP), slice(TOP + 16, TOP + 24), slice(TOP, TOP + 16)
ORDER = (4, 3, 5, 2, 6, 1, 7, 0)
ROUNDS = ((0, 1, 2, 3, 4, 5, 6),)
BATCHES = (2, 4, 6, 7)


def remote(src, dst, send, recv, where):
    return pltpu.make_async_remote_copy(
        src_ref=src, dst_ref=dst, send_sem=send, recv_sem=recv, device_id=where, device_id_type=MESH
    )


def gather(value, index, axis):
    return jnp.take_along_axis(value, index, axis=axis, mode="promise_in_bounds")


def restrict_block(ref, block, row, lane):
    halves = []
    for q in range(2):
        if 2 * block + q >= ref.shape[0]:
            halves.append(jnp.zeros((8, L), F32))
            continue
        pair = ref[2 * block + q, pl.ds(row, 8, stride=2), :] + ref[
            2 * block + q, pl.ds(row + 1, 8, stride=2), :
        ]
        pair = pair + pltpu.roll(pair, L - 1, 1)
        halves.append(gather(pair, (2 * lane) % L, 1))
    return jnp.where(lane < H, halves[0], halves[1]) * 0.25


def fluxes(u, right, up, down, cx, cx_up, cy, carry, lane):
    flow = cy * (right - u)
    turned = pltpu.roll(flow, 1, 1)
    west = jnp.where(lane == 0, carry, turned)
    total = cx * (down - u) - cx_up * (u - up)
    return total + flow - west, turned


def fine_step(pairs, co, first, tiles, last_strip, last_window):
    cx, cy, source = (co.at[i] for i in range(3))
    blocks = co.shape[1]
    lane = lax.broadcasted_iota(jnp.int32, (8, L), 1)
    row = lax.broadcasted_iota(jnp.int32, (8, L), 0)
    zero = jnp.zeros((8, L), F32)
    rows = [first + 8 * k for k in range(tiles)]
    below = [None if r + 8 <= TOP + 16 else (row + r >= TOP + 16) & last_strip for r in rows]
    beyond = (lane >= H) & last_window
    state = {}
    for n, (src, _) in enumerate(pairs):
        for k, r in enumerate(rows):
            u = src[0, r : r + 8, :]
            state[n, k] = (u, pltpu.roll(u, L - 1, 1), zero)
    for b in range(blocks):
        for n, (src, dst) in enumerate(pairs):
            for k, r in enumerate(rows):
                u, ru, turned = state[n, k]
                nxt, rn = zero, zero
                if b + 1 < blocks:
                    nxt = src[b + 1, r : r + 8, :]
                    rn = pltpu.roll(nxt, L - 1, 1)
                right = jnp.where(lane == L - 1, rn, ru)
                change, turned = fluxes(
                    u, right, src[b, r - 1 : r + 7, :], src[b, r + 1 : r + 9, :],
                    cx[b, r : r + 8, :], cx[b, r - 1 : r + 7, :], cy[b, r : r + 8, :], turned, lane,
                )
                out = u + change + source[b, r : r + 8, :]
                drop = below[k]
                if b + 1 == blocks:
                    drop = beyond if drop is None else drop | beyond
                if drop is not None:
                    out = jnp.where(drop, 0.0, out)
                dst[b, r : r + 8, :] = out
                state[n, k] = (nxt, rn, turned)


def kernel(
    groups, strips, guess_in, cx_in, cy_in, source_in, inflow_in, out_hbm,
    stage, flow_stage, shifted, guess, relaxed, ua, ub, co, tcoarse, wsrc, win, rd, fa, fb, outw,
    in_sems, g_send, g_recv, c_send, c_recv, w_send, w_recv, d_send, d_recv, o_send, o_recv, own_sem,
):
    t = lax.axis_index("tm")
    s = lax.axis_index("space")
    has_up, has_down = s > 0, s < strips - 1
    last = groups - 1
    lane = lax.broadcasted_iota(jnp.int32, (8, L), 1)
    row = lax.broadcasted_iota(jnp.int32, (8, L), 0)
    zero = jnp.zeros((8, L), F32)
    blocks = shifted.shape[0] - 1
    width = blocks // groups
    cwidth = width // 2
    wb = width + 1
    sends = []

    def send(cond, copy):
        sends.append((cond, copy))

        @pl.when(cond)
        def _():
            copy.start()

    def drain():
        for cond, copy in sends:
            @pl.when(cond)
            def _(copy=copy):
                copy.wait_send()
        sends.clear()

    loads = [
        pltpu.make_async_copy(ref, stage.at[i], in_sems.at[i])
        for i, ref in enumerate((guess_in.at[0], cx_in, cy_in, source_in))
    ]
    loads.append(pltpu.make_async_copy(inflow_in, flow_stage, in_sems.at[4]))
    loads[0].start()

    barrier = pltpu.get_barrier_semaphore()
    for k in range(1, groups):
        pl.semaphore_signal(barrier, inc=1, device_id=(lax.rem(t + k, groups), s), device_id_type=MESH)

    @pl.when(has_up)
    def _():
        for k in range(groups):
            pl.semaphore_signal(barrier, inc=1, device_id=(lax.rem(t + k, groups), s - 1), device_id_type=MESH)

    @pl.when(has_down)
    def _():
        for k in range(groups):
            pl.semaphore_signal(barrier, inc=1, device_id=(lax.rem(t + k, groups), s + 1), device_id_type=MESH)

    near = 3 - jnp.where(has_up, 0, 1) - jnp.where(has_down, 0, 1)

    loads[0].wait()
    for load in loads[1:]:
        load.start()
    for r in range(0, 16, 8):
        before = zero
        for b in range(blocks):
            turned = pltpu.roll(stage[0, r : r + 8, b * L : (b + 1) * L], H, 1)
            shifted[b, r : r + 8, :] = jnp.where(lane < H, before, turned)
            before = turned
        shifted[blocks, r : r + 8, :] = jnp.where(lane < H, before, 0.0)

    def around(ref, a, rows, count, per):
        values = []
        for n in range(-1, count + 1):
            at = jnp.clip(t * per + n, 0, per * groups - 1)
            cols = pl.ds(pl.multiple_of(at * L, L), L)
            value = ref[rows, cols] if a is None else ref[a, rows, cols]
            if n < 0:
                value = jnp.where(t == 0, 0.0, value)
            if n == count:
                value = jnp.where(t == last, 0.0, value)
            values.append(value)
        return values

    pl.semaphore_wait(barrier, groups * near - 1)

    def guess_copy(g, k, part, where):
        c = lax.rem(t + k, groups)
        mine = (slice(0, 16), slice(8, 16), slice(0, 8))[part]
        there = (MAIN, UP, DOWN)[part]
        return remote(
            shifted.at[pl.ds(width * c, wb), mine, :], guess.at[g, :, there, :],
            g_send.at[part, k], g_recv.at[part, g], where or (c, s + (0, 1, -1)[part]),
        )

    for k in ORDER:
        send((t < last) & has_down, guess_copy(t, k, 1, None))
        send((t < last) & has_up, guess_copy(t, k, 2, None))
        if k > 0:
            send(t < last, guess_copy(t, k, 0, None))

    for load in loads[1:]:
        load.wait()
    for a in range(3):
        for r in range(0, 16, 8):
            turned = [pltpu.roll(v, H, 1) for v in around(stage, 1 + a, slice(r, r + 8), width, width)]
            for i in range(wb):
                co[a, i, TOP + r : TOP + r + 8, :] = jnp.where(lane < H, turned[i], turned[i + 1])
    send(has_down, remote(co.at[:, :, TOP + 8 : TOP + 16, :], co.at[:, :, UP, :], c_send.at[0], c_recv.at[0], (t, s + 1)))
    send(has_up, remote(co.at[:, :, TOP : TOP + 8, :], co.at[:, :, DOWN, :], c_send.at[1], c_recv.at[1], (t, s - 1)))

    turned = [pltpu.roll(v, H // 2, 1) for v in around(flow_stage, None, slice(0, 8), cwidth, cwidth)]
    for i in range(cwidth + 1):
        value = jnp.where(lane < H // 2, turned[i], turned[i + 1])
        for a in range(3):
            if a > 0:
                value = restrict_block(co.at[a - 1], i, TOP, lane)
            wsrc[a, i, :, :] = value
            win[a, i, 16:24, :] = value
    w_down = remote(wsrc, win.at[:, :, 8:16, :], w_send.at[0], w_recv.at[0], (t, s + 1))
    w_up = remote(wsrc, win.at[:, :, 24:32, :], w_send.at[1], w_recv.at[1], (t, s - 1))
    send(has_down, w_down)
    send(has_up, w_up)

    def clear(fine, coarse, halo):
        for i in range(wb):
            for a in range(3):
                co[a, i, fine, :] = zero
            for g in range(last):
                guess[g, i, fine, :] = zero
        for i in range(cwidth + 1):
            for a in range(3):
                win[a, i, coarse, :] = zero
            for j in range(groups):
                rd[j, i, halo, :] = zero

    @pl.when(~has_up)
    def _():
        clear(UP, slice(8, 16), slice(0, 8))

    @pl.when(~has_down)
    def _():
        clear(DOWN, slice(24, 32), slice(16, 24))

    @pl.when(t < last)
    def _():
        for i in range(wb):
            guess[t, i, MAIN, :] = shifted[width * t + i, :, :]

    @pl.when(has_up)
    def _():
        remote(co.at[:, :, TOP + 8 : TOP + 16, :], co.at[:, :, UP, :], c_send.at[0], c_recv.at[0], (t, s)).wait_recv()
        remote(wsrc, win.at[:, :, 8:16, :], w_send.at[0], w_recv.at[0], (t, s)).wait_recv()

    @pl.when(has_down)
    def _():
        remote(co.at[:, :, TOP : TOP + 8, :], co.at[:, :, DOWN, :], c_send.at[1], c_recv.at[1], (t, s)).wait_recv()
        remote(wsrc, win.at[:, :, 24:32, :], w_send.at[1], w_recv.at[1], (t, s)).wait_recv()

    def arrive(g):
        @pl.when(has_up)
        def _():
            guess_copy(g, 0, 1, (t, s)).wait_recv()

        @pl.when(has_down)
        def _():
            guess_copy(g, 0, 2, (t, s)).wait_recv()

        @pl.when(t != g)
        def _():
            guess_copy(g, 0, 0, (t, s)).wait_recv()

    step = functools.partial(fine_step, co=co, last_strip=~has_down, last_window=t == last)
    for part in ROUNDS:
        for k in part:
            arrive(k)
        g0, r0 = [guess.at[k] for k in part], [relaxed.at[k] for k in part]
        a0, b0 = [ua.at[n] for n in range(len(part))], [ub.at[n] for n in range(len(part))]
        first_pass_done = False
        for src, dst, first, tiles in (
            (g0, a0, -8, 4), (a0, b0, -8, 4), (b0, a0, -8, 4), (a0, r0, -4, 3),
            (r0, a0, -4, 3), (a0, b0, -4, 3), (b0, a0, -4, 3), (a0, b0, 0, 2),
        ):
            both = list(zip(src, dst))
            if src is r0 or first_pass_done:
                first_pass_done = True
                both = [pair for k, pair in zip(part, both) if k < last - 1]
            step(both, first=TOP + first, tiles=tiles)
        for i in range(cwidth + 1):
            for n, k in enumerate(part):
                o = k + 1
                tcoarse[o, i, 7:15, :] = restrict_block(relaxed.at[k], i, TOP - 2, lane)
                value = restrict_block(relaxed.at[k], i, TOP + 2, lane)
                tcoarse[o, i, 9:17, :] = jnp.where((row == 7) & ~has_down, 0.0, value)
        turned = {k: zero for k in part}
        for i in range(cwidth + 1):
            for n, k in enumerate(part):
                o = k + 1
                if o == last:
                    continue
                u = tcoarse[o, i, 8:16, :]
                rn = pltpu.roll(tcoarse[o, i + 1, 8:16, :], L - 1, 1) if i < cwidth else zero
                right = jnp.where(lane == L - 1, rn, pltpu.roll(u, L - 1, 1))
                change, turned[k] = fluxes(
                    u, right, tcoarse[o, i, 7:15, :], tcoarse[o, i, 9:17, :],
                    win[1, i, 16:24, :], win[1, i, 15:23, :], win[2, i, 16:24, :], turned[k], lane,
                )
                rd[o, i, 8:16, :] = restrict_block(ub.at[n], i, TOP, lane) - (u + change)
    for i in range(cwidth + 1):
        rd[0, i, 8:16, :] = tcoarse[1, i, 8:16, :]

    def d_copy(j, part, where):
        halo = last - 1 - j
        mine = (slice(16 - halo, 16), slice(8, 8 + halo))[part]
        there = (slice(8 - halo, 8), slice(16, 16 + halo))[part]
        both = slice(j, j + 2)
        return remote(rd.at[both, :, mine, :], rd.at[both, :, there, :], d_send.at[part, j], d_recv.at[part, j], where)

    for j in range(0, last - 1, 2):
        send(has_down, d_copy(j, 0, (t, s + 1)))
        send(has_up, d_copy(j, 1, (t, s - 1)))

    for g in range(groups):
        k = max(g - 1, 0)
        ref = relaxed if g > 0 else guess
        for r in range(0, 16, 8):
            turned = [pltpu.roll(ref[k, i, TOP + r : TOP + r + 8, :], H, 1) for i in range(wb)]
            for i in range(width):
                outw[g, r : r + 8, i * L : (i + 1) * L] = jnp.where(lane < H, turned[i], turned[i + 1])

    def finish(g, error):
        for i in range(width):
            base = H // 2 + H * i
            at = base % L + lane // 2
            wide = gather(error[base // L], at % L, 1)
            if base % L + H > L:
                wide = jnp.where(at < L, wide, gather(error[base // L + 1], at % L, 1))
            for p in range(2):
                tall = gather(wide, row // 2 + 4 * p, 0)
                rows, cols = slice(8 * p, 8 * p + 8), slice(i * L, (i + 1) * L)
                outw[g, rows, cols] = outw[g, rows, cols] + tall

    def send_windows(start, stop):
        for g in range(start, stop):
            send(t != g, out_copy(g, t, (g, s)))

            @pl.when(t == g)
            def _():
                own_copy(g).start()

    def out_copy(g, c, where):
        cols = pl.ds(pl.multiple_of(c * (width * L), L), width * L)
        return remote(outw.at[g], out_hbm.at[0, :, cols], o_send.at[g], o_recv.at[c], where)

    def own_copy(g):
        cols = pl.ds(pl.multiple_of(t * (width * L), L), width * L)
        return pltpu.make_async_copy(outw.at[g], out_hbm.at[0, :, cols], own_sem)

    finish(0, [win[0, i, 16:24, :] for i in range(cwidth + 1)])
    send_windows(0, 1)

    keep = {}
    for k in range(3):
        for i in range(cwidth + 1):
            bad = jnp.broadcast_to(~has_down, (8, L)) if k == 2 else None
            if i == cwidth:
                beyond = (lane >= H // 2) & (t == last)
                bad = beyond if bad is None else bad | beyond
            keep[k, i] = bad
    for j in range(0, last - 1, 2):
        @pl.when(has_up)
        def _():
            d_copy(j, 0, (t, s)).wait_recv()

        @pl.when(has_down)
        def _():
            d_copy(j, 1, (t, s)).wait_recv()

    now, later = win.at[0], fa
    for g in range(1, groups):
        j = g - 1
        error = []
        for k in range(3):
            if g == last and k != 1:
                continue
            r = 8 + 8 * k
            turned = zero
            for i in range(cwidth + 1):
                u = now[i, r : r + 8, :]
                rn = pltpu.roll(now[i + 1, r : r + 8, :], L - 1, 1) if i < cwidth else zero
                right = jnp.where(lane == L - 1, rn, pltpu.roll(u, L - 1, 1))
                change, turned = fluxes(
                    u, right, now[i, r - 1 : r + 7, :], now[i, r + 1 : r + 9, :],
                    win[1, i, r : r + 8, :], win[1, i, r - 1 : r + 7, :], win[2, i, r : r + 8, :], turned, lane,
                )
                value = u + change + rd[j, i, 8 * k : 8 * k + 8, :]
                if keep[k, i] is not None:
                    value = jnp.where(keep[k, i], 0.0, value)
                if g < last:
                    later[i, r : r + 8, :] = value
                if k == 1:
                    error.append(value - tcoarse[g, i, 8:16, :])
        now, later = later, (fb if later is fa else fa)
        finish(g, error)
        if g in BATCHES:
            send_windows(max([1] + [b + 1 for b in BATCHES if b < g]), g + 1)

    for c in range(groups):
        @pl.when(t != c)
        def _():
            out_copy(0, c, (t, s)).wait_recv()

    drain()
    own_copy(0).wait()


def solution(mesh):
    groups, strips = mesh.shape["tm"], mesh.shape["space"]

    def shards(guesses, cond_x, cond_y, source, inflow):
        _, rows, columns = guesses.shape
        blocks = columns // L
        assert rows == 16 and groups == 8 and blocks == 4 * groups
        vmem = lambda *shape: pltpu.VMEM(shape, F32)
        dma = lambda *shape: pltpu.SemaphoreType.DMA(shape)
        return pl.pallas_call(
            functools.partial(kernel, groups, strips),
            out_shape=jax.ShapeDtypeStruct(guesses.shape, F32),
            in_specs=[pl.BlockSpec(memory_space=pl.ANY)] * 5,
            out_specs=pl.BlockSpec(memory_space=pl.ANY),
            scratch_shapes=[
                vmem(4, rows, columns), vmem(rows // 2, columns // 2), vmem(blocks + 1, rows, L),
                vmem(groups - 1, 5, 48, L), vmem(groups - 1, 5, 48, L), vmem(groups - 1, 5, 48, L), vmem(groups - 1, 5, 48, L),
                vmem(3, 5, 48, L), vmem(groups, 3, 24, L), vmem(3, 3, 8, L), vmem(3, 3, 40, L),
                vmem(groups, 3, 24, L), vmem(3, 40, L), vmem(3, 40, L), vmem(groups, rows, 4 * L),
                dma(5), dma(3, groups), dma(3, groups), dma(2), dma(2), dma(2), dma(2),
                dma(2, groups), dma(2, groups), dma(groups), dma(groups), pltpu.SemaphoreType.DMA,
            ],
            compiler_params=pltpu.CompilerParams(
                collective_id=0, has_side_effects=True, vmem_limit_bytes=40 * 2**20
            ),
        )(*(pltpu.with_memory_space_constraint(x, pltpu.MemorySpace.HBM) for x in (guesses, cond_x, cond_y, source, inflow)))

    return jax.shard_map(
        shards,
        mesh=mesh,
        in_specs=(
            P("tm", "space", None),
            P("space", None),
            P("space", None),
            P("space", None),
            P("space", None),
        ),
        out_specs=P("tm", "space", None),
        check_vma=False,
    )
```
